32 devices in a mesh: section: 16 (over z, y, core), dp: 2 (over x).
Axes of the slice: x: 2, y: 2, z: 4, core: 2. Of those that a mesh axis runs over, the one named last changes fastest.
Arguments:
- section_states: bfloat16 [16, 4, 2, 16, 16, 512], P('section', None, 'dp'), may hold values from -6 to 6
- conv_kernels: bfloat16 [16, 2, 1152, 512], P('section'), may hold values from -0.1875 to 0.1875
- top_feed: bfloat16 [3, 4, 2, 16, 16, 512], P(None, None, 'dp'), may hold values from -6 to 6
Outputs:
- final_states: bfloat16 [16, 4, 2, 16, 16, 512], P('section', None, 'dp')
- kernel_grads: float32 [16, 2, 1152, 512], P('section', None, 'dp')
The draws below stay inside these ranges and needn't reach their ends.
All inputs are finite; a program needn't handle non-finite values.
Results may differ from the reference program's by a relative error of at most 0.024.
Values may be sent and summed in bfloat16 or wider, within the bound.
A program may use at most 128 MiB of HBM per device.

```python
import jax
import jax.numpy as jnp
from jax import lax

CH = 512
GW = 128
HW = 16
TICKS = 4
IMAGES = 2
SECTIONS = 16


def steps_of(rng, extent, split, least, largest):
    def one(axis_at, shards_of):
        heights = jax.random.uniform(jax.random.fold_in(jax.random.fold_in(rng, 6), axis_at), (shards_of,), jnp.float32, least / len(split), largest / len(split))
        return jnp.repeat(jnp.exp(heights), extent[axis_at] // shards_of).reshape((-1,) + (1,) * (len(extent) - axis_at - 1))

    level = one(*split[0])
    for cut in split[1:]:
        level = level * one(*cut)
    return level


def bell_draw(own_key, dims, deviation, bound, cuts=(), held_as=jnp.bfloat16):
    factor_of = steps_of(own_key, dims, cuts, -0.22, 0.18) if cuts else 1.0
    entries = jax.random.normal(own_key, dims, jnp.float32) * deviation * factor_of
    return jnp.minimum(jnp.maximum(entries, -bound), bound).astype(held_as)


def setup_inputs(seed: int = 0) -> dict:
    keys = jax.random.split(jax.random.key(seed), 4)
    return {
        "section_states": bell_draw(keys[0], (SECTIONS, 4, IMAGES, HW, HW, CH), 1.0, 6.0, ((0, 16), (2, 2))),
        "conv_kernels": bell_draw(keys[1], (SECTIONS, 2, 9 * GW, CH), (9 * GW) ** -0.5, 0.1875, ((0, 16),)),
        "top_feed": bell_draw(keys[2], (TICKS - 1, 4, IMAGES, HW, HW, CH), 1.0, 6.0, ((2, 2),)),
    }


def tap_stack(field):
    height = field.shape[1]
    width = field.shape[2]
    padded = jnp.pad(field, ((0, 0), (1, 1), (1, 1), (0, 0)))
    pieces = [padded[:, row_off:row_off + height, col_off:col_off + width, :] for row_off in range(3) for col_off in range(3)]
    stacked = jnp.stack(pieces, axis=3)
    return stacked.reshape(field.shape[0] * height * width, 9, field.shape[3] // GW, GW)

def smooth_grad(value):
    sigma = jax.nn.sigmoid(value)
    return sigma * (1.0 + value * (1.0 - sigma))

def kernel_view(kernel):
    return kernel.reshape(9, GW, kernel.shape[1] // GW, GW).astype(jnp.float32)

def conv_apply(taps, kernel, shape):
    result = jnp.einsum('nkgi,kigo->ngo', taps.astype(jnp.float32), kernel_view(kernel))
    return result.reshape(shape)

def conv_back(grad_field, kernel):
    taps = tap_stack(grad_field)[:, ::-1]
    result = jnp.einsum('nkgo,kigo->ngi', taps.astype(jnp.float32), kernel_view(kernel))
    return result.reshape(grad_field.shape)

def kernel_term(taps, grad_field):
    count = taps.shape[0]
    flat = grad_field.reshape(count, taps.shape[2], GW).astype(jnp.float32)
    result = jnp.einsum('nkgi,ngo->kigo', taps.astype(jnp.float32), flat)
    return result.reshape(9 * GW, taps.shape[2] * GW)

def coupling_back(state, kernels):
    shape = state.shape[1:]
    output_one = state[0].astype(jnp.float32)
    output_two = state[1].astype(jnp.float32)
    grad_one = state[2]
    grad_two = state[3]
    act_one = jax.nn.silu(output_one).astype(jnp.bfloat16)
    taps_one = tap_stack(act_one)
    input_two = (output_two - conv_apply(taps_one, kernels[1], shape)).astype(jnp.bfloat16)
    wide_two = input_two.astype(jnp.float32)
    act_two = jax.nn.silu(wide_two).astype(jnp.bfloat16)
    taps_two = tap_stack(act_two)
    input_one = (output_one - conv_apply(taps_two, kernels[0], shape)).astype(jnp.bfloat16)
    total_one = (grad_one.astype(jnp.float32) + conv_back(grad_two, kernels[1]) * smooth_grad(output_one)).astype(jnp.bfloat16)
    term_second = kernel_term(taps_one, grad_two)
    grad_input_two = (grad_two.astype(jnp.float32) + conv_back(total_one, kernels[0]) * smooth_grad(wide_two)).astype(jnp.bfloat16)
    term_first = kernel_term(taps_two, total_one)
    return (jnp.stack([input_one, input_two, total_one, grad_input_two]), jnp.stack([term_first, term_second]))

def run_section(pair):
    return coupling_back(pair[0], pair[1])

def reference(section_states, conv_kernels, top_feed):
    current = section_states
    total = jnp.zeros(conv_kernels.shape, jnp.float32)
    produced = section_states
    for tick in range(TICKS):
        produced, grads = lax.map(run_section, (current, conv_kernels))
        total = total + grads
        if tick + 1 < TICKS:
            current = jnp.concatenate([produced[1:], top_feed[tick][None]], axis=0)
    return (produced, total * (1.0 / (HW * HW)))
```

```python
import functools

import jax
import jax.numpy as jnp
from jax import lax
from jax.experimental import pallas as pl
from jax.experimental.pallas import tpu as pltpu
from jax.sharding import PartitionSpec as P

GW = 128
MESH = pl.DeviceIdType.MESH
PARTS = ((0, 1, 0), (3, 1, 0), (1, 2, 1))


def smooth_grad(value):
    sigma = jax.nn.sigmoid(value)
    return sigma * (1.0 + value * (1.0 - sigma))


def steps_in_order(groups, ticks):
    tuned = ((0, 0), (1, 0), (0, 1), (2, 0), (0, 2), (1, 1), (0, 3), (2, 1), (1, 2), (3, 0), (1, 3), (2, 2), (3, 1), (2, 3), (3, 2), (3, 3))
    if sorted(tuned) == [(group, tick) for group in range(groups) for tick in range(ticks)]:
        return tuned
    return [(group, tick) for tick in range(ticks) for group in range(groups)]


def fused_kernel(
    dims,
    states_ref,
    kernels_ref,
    feed_ref,
    final_ref,
    grads_ref,
    inbuf,
    outbuf,
    weights,
    flipped,
    padded,
    acc,
    gsend,
    gown,
    grecv,
    in_sem,
    send_sem,
    weight_sem,
    gsend_sem,
    grecv_sem,
):
    ticks, groups, images, height, width, share, shards = dims
    cells = height * width
    order = steps_in_order(groups, ticks)
    rows = images * cells
    pad = (height + 2) * width
    me = lax.axis_index("section")
    count = lax.axis_size("section")
    mine = lax.axis_index("dp")
    is_top = me == count - 1
    has_below = me > 0

    def lanes(group):
        start = group * GW
        return pl.ds(start if isinstance(group, int) else pl.multiple_of(start, GW), GW)

    def first_copy(group):
        return pltpu.make_async_copy(
            states_ref.at[:, :, lanes(group)], inbuf.at[0, group], in_sem.at[0, group, 0]
        )

    def feed_copies(tick, group):
        for first, size, part in PARTS:
            yield pltpu.make_async_copy(
                feed_ref.at[tick - 1, pl.ds(first, size), :, lanes(group)],
                inbuf.at[tick, group, pl.ds(first, size)],
                in_sem.at[tick, group, part],
            )

    def weight_copy(group, branch, column):
        return pltpu.make_async_copy(
            kernels_ref.at[branch, :, column, :, lanes(group)],
            weights.at[branch, group, :, :, pl.ds(column * GW, GW)],
            weight_sem.at[branch, group, column],
        )

    def below_copies(tick, group, wanted):
        for first, size, part in PARTS:
            if part == wanted:
                yield pltpu.make_async_remote_copy(
                    src_ref=outbuf.at[tick, group, pl.ds(first, size)],
                    dst_ref=inbuf.at[tick + 1, group, pl.ds(first, size)],
                    send_sem=send_sem.at[part],
                    recv_sem=in_sem.at[tick + 1, group, part],
                    device_id={"section": me - 1},
                    device_id_type=MESH,
                )

    def arrived(tick, group, part):
        pair = inbuf.at[tick, group, pl.ds(1, 2)]
        pltpu.make_async_copy(pair, pair, in_sem.at[tick, group, part]).wait()

    def share_copy(group, branch, offset):
        partner = lax.rem(mine + offset, shards)
        return pltpu.make_async_remote_copy(
            src_ref=gsend.at[branch, group, pl.ds(pl.multiple_of(partner * share, 16), share)],
            dst_ref=grecv.at[offset - 1, branch, group],
            send_sem=gsend_sem.at[offset - 1],
            recv_sem=grecv_sem.at[offset - 1, branch, group],
            device_id={"dp": partner},
            device_id_type=MESH,
        )

    barrier = pltpu.get_barrier_semaphore()

    @pl.when(has_below)
    def _():
        pl.semaphore_signal(barrier, inc=1, device_id={"section": me - 1}, device_id_type=MESH)

    @pl.when(jnp.logical_not(is_top))
    def _():
        pl.semaphore_signal(barrier, inc=1, device_id={"section": me + 1}, device_id_type=MESH)

    for offset in range(1, shards):
        pl.semaphore_signal(
            barrier,
            inc=1,
            device_id={"dp": lax.rem(mine + offset, shards)},
            device_id_type=MESH,
        )

    for group in range(groups):
        first_copy(group).start()
        for branch in (1, 0):
            for column in range(3):
                weight_copy(group, branch, column).start()

    @pl.when(is_top)
    def _():
        @pl.loop(1, ticks)
        def _(tick):
            for group in range(groups):
                for copy in feed_copies(tick, group):
                    copy.start()

    edge = jnp.zeros((4, images, width, GW), jnp.bfloat16)
    padded[:, :, 0:width, :] = edge
    padded[:, :, pad - width : pad, :] = edge

    greeted = jnp.where(has_below, 1, 0) + jnp.where(is_top, 0, 1) + (shards - 1)
    column = lax.rem(lax.broadcasted_iota(jnp.int32, (rows, GW), 0), width)
    at_left = column == 0
    at_right = column == width - 1
    chunk = GW if rows % GW == 0 and GW % width == 0 else rows
    lane_column = lax.rem(lax.broadcasted_iota(jnp.int32, (GW, chunk), 1), width)
    lane_left = lane_column == 0
    lane_right = lane_column == width - 1

    def put(slot, field):
        padded[slot, :, width : width + cells, :] = field.reshape(images, cells, GW)

    def slab(slot, order):
        return jnp.concatenate(
            [
                padded[slot, :, row * width : row * width + cells, :].reshape(rows, GW)
                for row in order
            ],
            axis=1,
        )

    def mix(slot, kernel):
        wide = lax.dot_general(
            slab(slot, (0, 1, 2)),
            kernel.reshape(3 * GW, 3 * GW),
            (((1,), (0,)), ((), ())),
            preferred_element_type=jnp.float32,
        )
        left = jnp.where(at_left, 0.0, pltpu.roll(wide[:, :GW], 1, 0))
        right = jnp.where(at_right, 0.0, pltpu.roll(wide[:, 2 * GW :], rows - 1, 0))
        return wide[:, GW : 2 * GW] + left + right

    def turned(field):
        flat = field.T
        parts = ([], [], [])
        for start in range(0, rows, chunk):
            piece = flat[:, start : start + chunk].astype(jnp.float32)
            left = jnp.where(lane_left, 0.0, pltpu.roll(piece, 1, 1))
            right = jnp.where(lane_right, 0.0, pltpu.roll(piece, chunk - 1, 1))
            parts[0].append(left.astype(jnp.bfloat16))
            parts[1].append(flat[:, start : start + chunk])
            parts[2].append(right.astype(jnp.bfloat16))
        return jnp.concatenate([jnp.concatenate(part, axis=1) for part in parts], axis=0)

    def add_term(branch, group, field, slot):
        acc[branch, group] += lax.dot_general(
            turned(field),
            slab(slot, (2, 1, 0)),
            (((1,), (0,)), ((), ())),
            preferred_element_type=jnp.float32,
        )

    def hand_on(branch, group):
        for k in range(9):
            down, side = divmod(k, 3)
            block = acc[
                branch, group, side * GW : (side + 1) * GW, down * GW : (down + 1) * GW
            ] * (1.0 / cells)
            gown[branch, group, k * GW : (k + 1) * GW, :] = block
            gsend[branch, group, k * GW : (k + 1) * GW, :] = block.astype(jnp.bfloat16)
        for offset in range(1, shards):
            share_copy(group, branch, offset).start()

    def prepare(branch, group):
        for column in range(3):
            weight_copy(group, branch, column).wait()
        for down in range(3):
            for side in range(3):
                flipped[branch, group, down, :, side * GW : (side + 1) * GW] = weights[
                    branch, group, 2 - down, :, (2 - side) * GW : (3 - side) * GW
                ].T
        acc[branch, group] = jnp.zeros((3 * GW, 3 * GW), jnp.float32)

    @pl.loop(0, ticks * groups)
    def _(step):
        word = jnp.int32(0)
        for place in range(0, len(order), 3):
            packed = 0
            for at, (at_group, at_tick) in enumerate(order[place : place + 3]):
                packed |= (at_group * 32 + at_tick) << (10 * at)
            word = jnp.where(step >= place, packed, word)
        entry = lax.shift_right_logical(word, 10 * lax.rem(step, 3))
        tick = entry & 31
        group = lax.shift_right_logical(entry, 5) & 31
        is_first = tick == 0
        is_last = tick == ticks - 1
        sending = jnp.logical_and(jnp.logical_not(is_last), has_below)

        def give(part):
            for copy in below_copies(tick, group, part):
                copy.start()

        def finish(streams):
            for stream in streams:
                final_ref[stream, :, lanes(group)] = outbuf[tick, group, stream]

        @pl.when(is_first)
        def _():
            first_copy(group).wait()
            prepare(1, group)

        @pl.when(jnp.logical_not(is_first))
        def _():
            arrived(tick, group, 0)

        one = inbuf[tick, group, 0].astype(jnp.float32)
        act_one = jax.nn.silu(one).astype(jnp.bfloat16)
        put(0, act_one)
        put(1, inbuf[tick, group, 3])
        add_term(1, group, act_one, 1)
        mixed_one = mix(0, weights[1, group])
        mixed_two = mix(1, flipped[1, group]) * smooth_grad(one)

        @pl.when(step == 0)
        def _():
            pl.semaphore_wait(barrier, greeted)

        @pl.when(is_last)
        def _():
            hand_on(1, group)

        @pl.when(jnp.logical_not(is_first))
        def _():
            arrived(tick, group, 1)

        input_two = (inbuf[tick, group, 1].astype(jnp.float32) - mixed_one).astype(jnp.bfloat16)
        outbuf[tick, group, 1] = input_two
        total_one = (inbuf[tick, group, 2].astype(jnp.float32) + mixed_two).astype(jnp.bfloat16)
        outbuf[tick, group, 2] = total_one

        @pl.when(is_first)
        def _():
            @pl.when(sending)
            def _():
                give(1)

            prepare(0, group)

        wide_two = input_two.astype(jnp.float32)
        act_two = jax.nn.silu(wide_two).astype(jnp.bfloat16)
        put(2, act_two)
        put(3, total_one)
        outbuf[tick, group, 0] = (
            inbuf[tick, group, 0].astype(jnp.float32) - mix(2, weights[0, group])
        ).astype(jnp.bfloat16)
        outbuf[tick, group, 3] = (
            inbuf[tick, group, 3].astype(jnp.float32)
            + mix(3, flipped[0, group]) * smooth_grad(wide_two)
        ).astype(jnp.bfloat16)

        @pl.when(sending)
        def _():
            give(0)

            @pl.when(jnp.logical_not(is_first))
            def _():
                give(1)

        add_term(0, group, act_two, 3)

        @pl.when(is_last)
        def _():
            hand_on(0, group)
            finish(range(4))

    @pl.loop(0, groups)
    def _(group):
        for branch in (1, 0):
            total = gown[branch, group, pl.ds(pl.multiple_of(mine * share, 16), share), :]
            for offset in range(1, shards):
                share_copy(group, branch, offset).wait_recv()
                total = total + grecv[offset - 1, branch, group].astype(jnp.float32)
            grads_ref[branch, :, lanes(group)] = total

    for offset in range(1, shards):
        every = gsend.at[:, :, pl.ds(0, share)]
        pltpu.make_async_copy(every, every, gsend_sem.at[offset - 1]).wait()

    @pl.when(has_below)
    def _():
        for part in range(2):
            every = outbuf.at[pl.ds(0, ticks - 1), :, pl.ds(0, 2)]
            pltpu.make_async_copy(every, every, send_sem.at[part]).wait()


def on_device(section_states, conv_kernels, top_feed):
    _, _, images, height, width, chans = section_states.shape
    ticks = top_feed.shape[0] + 1
    groups = chans // GW
    shards = lax.axis_size("dp")
    taps_rows = conv_kernels.shape[2]
    share = taps_rows // shards
    rows = images * height * width
    states = section_states.reshape(4, rows, chans)
    feed = top_feed.reshape(ticks - 1, 4, rows, chans)
    dims = (ticks, groups, images, height, width, share, shards)
    anywhere = pl.BlockSpec(memory_space=pltpu.HBM)
    dma = pltpu.SemaphoreType.DMA
    final, grads = pl.pallas_call(
        functools.partial(fused_kernel, dims),
        out_shape=(
            pltpu.VMEM((4, rows, chans), jnp.bfloat16),
            pltpu.VMEM((2, share, chans), jnp.float32),
        ),
        in_specs=[anywhere] * 3,
        out_specs=[pl.BlockSpec(memory_space=pltpu.VMEM)] * 2,
        scratch_shapes=[
            pltpu.VMEM((ticks, groups, 4, rows, GW), jnp.bfloat16),
            pltpu.VMEM((ticks, groups, 4, rows, GW), jnp.bfloat16),
            pltpu.VMEM((2, groups, 3, GW, 3 * GW), jnp.bfloat16),
            pltpu.VMEM((2, groups, 3, GW, 3 * GW), jnp.bfloat16),
            pltpu.VMEM((4, images, (height + 2) * width, GW), jnp.bfloat16),
            pltpu.VMEM((2, groups, 3 * GW, 3 * GW), jnp.float32),
            pltpu.VMEM((2, groups, taps_rows, GW), jnp.bfloat16),
            pltpu.VMEM((2, groups, taps_rows, GW), jnp.float32),
            pltpu.VMEM((max(shards - 1, 1), 2, groups, share, GW), jnp.bfloat16),
            dma((ticks, groups, 2)),
            dma((2,)),
            dma((2, groups, 3)),
            dma((max(shards - 1, 1),)),
            dma((max(shards - 1, 1), 2, groups)),
        ],
        compiler_params=pltpu.CompilerParams(
            collective_id=0, has_side_effects=True, vmem_limit_bytes=56 * 1024 * 1024
        ),
    )(states, conv_kernels.reshape(2, 3, 3, GW, chans), feed)
    return (
        final.reshape(section_states.shape),
        grads.reshape(1, 2, share, chans),
    )


def solution(mesh):
    return jax.shard_map(
        on_device,
        mesh=mesh,
        in_specs=(
            P("section", None, "dp", None, None, None),
            P("section", None, None, None),
            P(None, None, "dp", None, None, None),
        ),
        out_specs=(P("section", None, "dp", None, None, None), P("section", None, "dp", None)),
        check_vma=False,
    )
```

```python
import functools

import jax
import jax.numpy as jnp
from jax import lax
from jax.experimental import pallas as pl
from jax.experimental.pallas import tpu as pltpu
from jax.sharding import PartitionSpec as P

GW = 128
MESH = pl.DeviceIdType.MESH
PARTS = ((0, 1, 0), (3, 1, 0), (1, 2, 1))


def smooth_grad(value):
    sigma = jax.nn.sigmoid(value)
    return sigma * (1.0 + value * (1.0 - sigma))


def steps_in_order(groups, ticks):
    tuned = ((0, 0), (1, 0), (0, 1), (2, 0), (0, 2), (1, 1), (0, 3), (2, 1), (1, 2), (3, 0), (1, 3), (2, 2), (3, 1), (2, 3), (3, 2), (3, 3))
    if sorted(tuned) == [(group, tick) for group in range(groups) for tick in range(ticks)]:
        return tuned
    return [(group, tick) for tick in range(ticks) for group in range(groups)]


def fused_kernel(
    dims,
    states_ref,
    kernels_ref,
    feed_ref,
    final_ref,
    grads_ref,
    inbuf,
    outbuf,
    weights,
    flipped,
    padded,
    acc,
    gsend,
    gown,
    grecv,
    in_sem,
    send_sem,
    weight_sem,
    gsend_sem,
    grecv_sem,
):
    ticks, groups, images, height, width, share, shards = dims
    cells = height * width
    order = steps_in_order(groups, ticks)
    rows = images * cells
    pad = (height + 2) * width
    me = lax.axis_index("section")
    count = lax.axis_size("section")
    mine = lax.axis_index("dp")
    is_top = me == count - 1
    has_below = me > 0

    def lanes(group):
        start = group * GW
        return pl.ds(start if isinstance(group, int) else pl.multiple_of(start, GW), GW)

    def first_copy(group):
        return pltpu.make_async_copy(
            states_ref.at[:, :, lanes(group)], inbuf.at[0, group], in_sem.at[0, group, 0]
        )

    def feed_copies(tick, group):
        for first, size, part in PARTS:
            yield pltpu.make_async_copy(
                feed_ref.at[tick - 1, pl.ds(first, size), :, lanes(group)],
                inbuf.at[tick, group, pl.ds(first, size)],
                in_sem.at[tick, group, part],
            )

    def weight_copy(group, branch, column):
        row, place = ((0, 0), (0, 1), (3, 1))[column]
        return pltpu.make_async_copy(
            kernels_ref.at[branch, :, column, :, lanes(group)],
            weights.at[branch, group, pl.ds(row, 3), :, pl.ds(place * GW, GW)],
            weight_sem.at[branch, group],
        )

    def weights_arrived(group, branch):
        whole = kernels_ref.at[branch, :, :, :, lanes(group)]
        pltpu.make_async_copy(whole, whole, weight_sem.at[branch, group]).wait()

    def below_copy(tick, group, first, size, part):
        return pltpu.make_async_remote_copy(
            src_ref=outbuf.at[tick, group, pl.ds(first, size)],
            dst_ref=inbuf.at[tick + 1, group, pl.ds(first, size)],
            send_sem=send_sem.at[part],
            recv_sem=in_sem.at[tick + 1, group, part],
            device_id={"section": me - 1},
            device_id_type=MESH,
        )

    def arrived(tick, group, part):
        pair = inbuf.at[tick, group, pl.ds(1, 2)]
        pltpu.make_async_copy(pair, pair, in_sem.at[tick, group, part]).wait()

    def share_copy(group, branch, offset):
        partner = lax.rem(mine + offset, shards)
        return pltpu.make_async_remote_copy(
            src_ref=gsend.at[branch, group, pl.ds(pl.multiple_of(partner * share, 16), share)],
            dst_ref=grecv.at[offset - 1, branch, group],
            send_sem=gsend_sem.at[offset - 1],
            recv_sem=grecv_sem.at[offset - 1, branch, group],
            device_id={"dp": partner},
            device_id_type=MESH,
        )

    barrier = pltpu.get_barrier_semaphore()

    @pl.when(has_below)
    def _():
        pl.semaphore_signal(barrier, inc=1, device_id={"section": me - 1}, device_id_type=MESH)

    @pl.when(jnp.logical_not(is_top))
    def _():
        pl.semaphore_signal(barrier, inc=1, device_id={"section": me + 1}, device_id_type=MESH)

    for offset in range(1, shards):
        pl.semaphore_signal(
            barrier,
            inc=1,
            device_id={"dp": lax.rem(mine + offset, shards)},
            device_id_type=MESH,
        )

    for group in range(groups):
        first_copy(group).start()
        for branch in (1, 0):
            for column in range(3):
                weight_copy(group, branch, column).start()

    @pl.when(is_top)
    def _():
        @pl.loop(1, ticks)
        def _(tick):
            for group in range(groups):
                for copy in feed_copies(tick, group):
                    copy.start()

    edge = jnp.zeros((4, 2, images, width, GW), jnp.bfloat16)
    padded[:, :, :, 0:width, :] = edge
    padded[:, :, :, pad - width : pad, :] = edge
    blank = jnp.zeros((3, GW, GW), jnp.bfloat16)

    greeted = jnp.where(has_below, 1, 0) + jnp.where(is_top, 0, 1) + (shards - 1)
    column = lax.rem(lax.broadcasted_iota(jnp.int32, (rows, GW), 0), width)
    at_left = column == 0
    at_right = column == width - 1
    chunk = GW if rows % GW == 0 and GW % width == 0 else rows
    lane_column = lax.rem(lax.broadcasted_iota(jnp.int32, (GW, chunk), 1), width)
    lane_left = lane_column == 0
    lane_right = lane_column == width - 1

    def put(slot, field):
        wide = field.astype(jnp.float32)
        ahead = jnp.where(at_right, 0.0, pltpu.roll(wide, rows - 1, 0)).astype(jnp.bfloat16)
        for place, piece in enumerate((field, ahead)):
            padded[slot, place, :, width : width + cells, :] = piece.reshape(images, cells, GW)

    def slab(slot, places, order):
        return jnp.concatenate(
            [
                padded[slot, place, :, row * width : row * width + cells, :].reshape(rows, GW)
                for place in places
                for row in order
            ],
            axis=1,
        )

    def mix(slot, kernel):
        wide = lax.dot_general(
            slab(slot, (0, 1), (0, 1, 2)),
            kernel.reshape(6 * GW, 2 * GW),
            (((1,), (0,)), ((), ())),
            preferred_element_type=jnp.float32,
        )
        return wide[:, GW:] + jnp.where(at_left, 0.0, pltpu.roll(wide[:, :GW], 1, 0))

    def turned(field):
        flat = field.T
        parts = ([], [], [])
        for start in range(0, rows, chunk):
            piece = flat[:, start : start + chunk].astype(jnp.float32)
            left = jnp.where(lane_left, 0.0, pltpu.roll(piece, 1, 1))
            right = jnp.where(lane_right, 0.0, pltpu.roll(piece, chunk - 1, 1))
            parts[0].append(left.astype(jnp.bfloat16))
            parts[1].append(flat[:, start : start + chunk])
            parts[2].append(right.astype(jnp.bfloat16))
        return jnp.concatenate([jnp.concatenate(part, axis=1) for part in parts], axis=0)

    def term_of(field, slot):
        return lax.dot_general(
            turned(field),
            slab(slot, (0,), (2, 1, 0)),
            (((1,), (0,)), ((), ())),
            preferred_element_type=jnp.float32,
        )

    def hand_on(branch, group, field, slot):
        term = term_of(field, slot)
        for k in range(9):
            down, side = divmod(k, 3)
            here = (
                slice(side * GW, (side + 1) * GW),
                slice(down * GW, (down + 1) * GW),
            )
            block = (acc[(branch, group, *here)] + term[here]) * (1.0 / cells)
            gown[branch, group, k * GW : (k + 1) * GW, :] = block
            gsend[branch, group, k * GW : (k + 1) * GW, :] = block.astype(jnp.bfloat16)
        for offset in range(1, shards):
            share_copy(group, branch, offset).start()

    def prepare(branch, group):
        weights[branch, group, 3:6, :, 0:GW] = blank
        flipped[branch, group, 3:6, :, 0:GW] = blank
        for down in range(3):
            for side, (row, place) in enumerate(((0, 0), (0, 1), (3, 1))):
                from_row, from_place = ((0, 0), (0, 1), (3, 1))[2 - side]
                flipped[branch, group, row + down, :, place * GW : (place + 1) * GW] = weights[
                    branch, group, from_row + 2 - down, :, from_place * GW : (from_place + 1) * GW
                ].T

    def section(step, tick, group, first, last):
        def give(*copies):
            @pl.when(has_below)
            def _():
                for copy in copies:
                    below_copy(tick, group, *copy).start()

        def keep(stream, value):
            if last:
                final_ref[stream, :, lanes(group)] = value
            else:
                outbuf[tick, group, stream] = value

        def stream(at):
            return inbuf[tick, group, at].astype(jnp.float32)

        if first:
            first_copy(group).wait()
            weights_arrived(group, 1)
        else:
            arrived(tick, group, 0)
        one = stream(0)
        act_one = jax.nn.silu(one).astype(jnp.bfloat16)
        put(0, act_one)
        put(1, inbuf[tick, group, 3])
        if last:
            hand_on(1, group, act_one, 1)
        mixed_one = mix(0, weights[1, group])
        if first:
            input_two = (stream(1) - mixed_one).astype(jnp.bfloat16)
            keep(1, input_two)

            @pl.when(step == 0)
            def _():
                pl.semaphore_wait(barrier, greeted)

            give((1, 1, 1))
            prepare(1, group)
        mixed_two = mix(1, flipped[1, group]) * smooth_grad(one)
        if not first:
            arrived(tick, group, 1)
            input_two = (stream(1) - mixed_one).astype(jnp.bfloat16)
            keep(1, input_two)
        total_one = (stream(2) + mixed_two).astype(jnp.bfloat16)
        keep(2, total_one)
        if first:
            give((2, 1, 1))
            weights_arrived(group, 0)
            prepare(0, group)
        wide_two = input_two.astype(jnp.float32)
        act_two = jax.nn.silu(wide_two).astype(jnp.bfloat16)
        put(2, act_two)
        put(3, total_one)
        if last:
            hand_on(0, group, act_two, 3)
        keep(0, (stream(0) - mix(2, weights[0, group])).astype(jnp.bfloat16))
        keep(
            3,
            (stream(3) + mix(3, flipped[0, group]) * smooth_grad(wide_two)).astype(jnp.bfloat16),
        )
        if first:
            give((0, 1, 0), (3, 1, 0))
            acc[1, group] = term_of(act_one, 1)
            acc[0, group] = term_of(act_two, 3)
        elif not last:
            give((0, 1, 0), (3, 1, 0), (1, 2, 1))
            acc[1, group] += term_of(act_one, 1)
            acc[0, group] += term_of(act_two, 3)

    @pl.loop(0, ticks * groups)
    def _(step):
        word = jnp.int32(0)
        for place in range(0, len(order), 3):
            packed = 0
            for at, (at_group, at_tick) in enumerate(order[place : place + 3]):
                packed |= (at_group * 32 + at_tick) << (10 * at)
            word = jnp.where(step >= place, packed, word)
        entry = lax.shift_right_logical(word, 10 * lax.rem(step, 3))
        tick = entry & 31
        group = lax.shift_right_logical(entry, 5) & 31

        @pl.when(tick == 0)
        def _():
            section(step, 0, group, True, False)

        @pl.when(jnp.logical_and(tick > 0, tick < ticks - 1))
        def _():
            section(step, tick, group, False, False)

        @pl.when(tick == ticks - 1)
        def _():
            section(step, ticks - 1, group, False, True)

    @pl.loop(0, groups)
    def _(group):
        for branch in (1, 0):
            total = gown[branch, group, pl.ds(pl.multiple_of(mine * share, 16), share), :]
            for offset in range(1, shards):
                share_copy(group, branch, offset).wait_recv()
                total = total + grecv[offset - 1, branch, group].astype(jnp.float32)
            grads_ref[branch, :, lanes(group)] = total

    for offset in range(1, shards):
        every = gsend.at[:, :, pl.ds(0, share)]
        pltpu.make_async_copy(every, every, gsend_sem.at[offset - 1]).wait()

    @pl.when(has_below)
    def _():
        for part in range(2):
            every = outbuf.at[pl.ds(0, ticks - 1), :, pl.ds(0, 2)]
            pltpu.make_async_copy(every, every, send_sem.at[part]).wait()


def write_kernel(final_ref, grads_ref, final_out, grads_out, sems):
    copies = [
        pltpu.make_async_copy(grads_ref, grads_out, sems.at[0]),
        pltpu.make_async_copy(final_ref, final_out, sems.at[1]),
    ]
    for copy in copies:
        copy.start()
    for copy in copies:
        copy.wait()


def on_device(section_states, conv_kernels, top_feed):
    _, _, images, height, width, chans = section_states.shape
    ticks = top_feed.shape[0] + 1
    groups = chans // GW
    shards = lax.axis_size("dp")
    taps_rows = conv_kernels.shape[2]
    share = taps_rows // shards
    rows = images * height * width
    states = section_states.reshape(4, rows, chans)
    feed = top_feed.reshape(ticks - 1, 4, rows, chans)
    dims = (ticks, groups, images, height, width, share, shards)
    anywhere = pl.BlockSpec(memory_space=pltpu.HBM)
    dma = pltpu.SemaphoreType.DMA
    final, grads = pl.pallas_call(
        functools.partial(fused_kernel, dims),
        out_shape=(
            pltpu.VMEM((4, rows, chans), jnp.bfloat16),
            pltpu.VMEM((2, share, chans), jnp.float32),
        ),
        in_specs=[anywhere] * 3,
        out_specs=[pl.BlockSpec(memory_space=pltpu.VMEM)] * 2,
        scratch_shapes=[
            pltpu.VMEM((ticks, groups, 4, rows, GW), jnp.bfloat16),
            pltpu.VMEM((ticks, groups, 4, rows, GW), jnp.bfloat16),
            pltpu.VMEM((2, groups, 6, GW, 2 * GW), jnp.bfloat16),
            pltpu.VMEM((2, groups, 6, GW, 2 * GW), jnp.bfloat16),
            pltpu.VMEM((4, 2, images, (height + 2) * width, GW), jnp.bfloat16),
            pltpu.VMEM((2, groups, 3 * GW, 3 * GW), jnp.float32),
            pltpu.VMEM((2, groups, taps_rows, GW), jnp.bfloat16),
            pltpu.VMEM((2, groups, taps_rows, GW), jnp.float32),
            pltpu.VMEM((max(shards - 1, 1), 2, groups, share, GW), jnp.bfloat16),
            dma((ticks, groups, 2)),
            dma((2,)),
            dma((2, groups)),
            dma((max(shards - 1, 1),)),
            dma((max(shards - 1, 1), 2, groups)),
        ],
        compiler_params=pltpu.CompilerParams(
            collective_id=0, has_side_effects=True, vmem_limit_bytes=56 * 1024 * 1024
        ),
    )(states, conv_kernels.reshape(2, 3, 3, GW, chans), feed)
    final, grads = pl.pallas_call(
        write_kernel,
        out_shape=(
            jax.ShapeDtypeStruct(final.shape, final.dtype),
            jax.ShapeDtypeStruct(grads.shape, grads.dtype),
        ),
        in_specs=[pl.BlockSpec(memory_space=pltpu.VMEM)] * 2,
        out_specs=[anywhere] * 2,
        scratch_shapes=[dma((2,))],
        compiler_params=pltpu.CompilerParams(vmem_limit_bytes=1024 * 1024),
    )(final, grads)
    return (
        final.reshape(section_states.shape),
        grads.reshape(1, 2, share, chans),
    )


def solution(mesh):
    return jax.shard_map(
        on_device,
        mesh=mesh,
        in_specs=(
            P("section", None, "dp", None, None, None),
            P("section", None, None, None),
            P(None, None, "dp", None, None, None),
        ),
        out_specs=(P("section", None, "dp", None, None, None), P("section", None, "dp", None)),
        check_vma=False,
    )
```

```python
import functools

import jax
import jax.numpy as jnp
from jax import lax
from jax.experimental import pallas as pl
from jax.experimental.pallas import tpu as pltpu
from jax.sharding import PartitionSpec as P

GW = 128
MESH = pl.DeviceIdType.MESH
PARTS = ((0, 1, 0), (3, 1, 0), (1, 2, 1))


def smooth_grad(value):
    sigma = jax.nn.sigmoid(value)
    return sigma * (1.0 + value * (1.0 - sigma))


def steps_in_order(groups, ticks):
    tuned = ((0, 0), (0, 1), (1, 0), (0, 2), (1, 1), (0, 3), (2, 0), (1, 2), (2, 1), (1, 3), (3, 0), (2, 2), (3, 1), (2, 3), (3, 2), (3, 3))
    if sorted(tuned) == [(group, tick) for group in range(groups) for tick in range(ticks)]:
        return tuned
    return [(group, tick) for tick in range(ticks) for group in range(groups)]


def fused_kernel(
    dims,
    states_ref,
    kernels_ref,
    feed_ref,
    final_ref,
    grads_ref,
    inbuf,
    outbuf,
    weights,
    flipped,
    padded,
    acc,
    gsend,
    gown,
    grecv,
    in_sem,
    send_sem,
    weight_sem,
    turn_sem,
    gsend_sem,
    grecv_sem,
):
    ticks, groups, images, height, width, share, shards = dims
    cells = height * width
    order = steps_in_order(groups, ticks)
    rows = images * cells
    pad = (height + 2) * width
    me = lax.axis_index("section")
    count = lax.axis_size("section")
    mine = lax.axis_index("dp")
    is_top = me == count - 1
    lower = jnp.logical_and(lax.rem(me, 2) == 0, me < count - 1)
    upper = lax.rem(me, 2) == 1
    has_below = me > 0

    def lanes(group):
        start = group * GW
        return pl.ds(start if isinstance(group, int) else pl.multiple_of(start, GW), GW)

    def first_copy(group):
        return pltpu.make_async_copy(
            states_ref.at[:, :, lanes(group)], inbuf.at[0, group], in_sem.at[0, group, 0]
        )

    def feed_copies(tick, group):
        for first, size, part in PARTS:
            yield pltpu.make_async_copy(
                feed_ref.at[tick - 1, pl.ds(first, size), :, lanes(group)],
                inbuf.at[tick, group, pl.ds(first, size)],
                in_sem.at[tick, group, part],
            )

    def weight_copy(group, branch, column):
        row, place = ((0, 0), (0, 1), (3, 1))[column]
        return pltpu.make_async_copy(
            kernels_ref.at[branch, :, column, :, lanes(group)],
            weights.at[branch, group, pl.ds(row, 3), :, pl.ds(place * GW, GW)],
            weight_sem.at[branch, group],
        )

    def weights_arrived(group, branch):
        whole = kernels_ref.at[branch, :, :, :, lanes(group)]
        pltpu.make_async_copy(whole, whole, weight_sem.at[branch, group]).wait()

    def below_copy(tick, group, first, size, part):
        return pltpu.make_async_remote_copy(
            src_ref=outbuf.at[tick, group, pl.ds(first, size)],
            dst_ref=inbuf.at[tick + 1, group, pl.ds(first, size)],
            send_sem=send_sem.at[part],
            recv_sem=in_sem.at[tick + 1, group, part],
            device_id={"section": me - 1},
            device_id_type=MESH,
        )

    def arrived(tick, group, part):
        pair = inbuf.at[tick, group, pl.ds(1, 2)]
        pltpu.make_async_copy(pair, pair, in_sem.at[tick, group, part]).wait()

    def share_copy(group, branch, offset):
        partner = lax.rem(mine + offset, shards)
        return pltpu.make_async_remote_copy(
            src_ref=gsend.at[branch, group, pl.ds(pl.multiple_of(partner * share, 16), share)],
            dst_ref=grecv.at[offset - 1, branch, group],
            send_sem=gsend_sem.at[offset - 1, branch],
            recv_sem=grecv_sem.at[offset - 1, branch, group],
            device_id={"dp": partner},
            device_id_type=MESH,
        )

    barrier = pltpu.get_barrier_semaphore()

    @pl.when(has_below)
    def _():
        pl.semaphore_signal(barrier, inc=1, device_id={"section": me - 1}, device_id_type=MESH)

    @pl.when(jnp.logical_not(is_top))
    def _():
        pl.semaphore_signal(barrier, inc=1, device_id={"section": me + 1}, device_id_type=MESH)

    for offset in range(1, shards):
        pl.semaphore_signal(
            barrier,
            inc=1,
            device_id={"dp": lax.rem(mine + offset, shards)},
            device_id_type=MESH,
        )

    for group in range(groups):
        first_copy(group).start()
        for branch in (1, 0):
            for column in range(3):
                weight_copy(group, branch, column).start()

    @pl.when(is_top)
    def _():
        @pl.loop(1, ticks)
        def _(tick):
            for group in range(groups):
                for copy in feed_copies(tick, group):
                    copy.start()

    edge = jnp.zeros((4, 2, images, width, GW), jnp.bfloat16)
    padded[:, :, :, 0:width, :] = edge
    padded[:, :, :, pad - width : pad, :] = edge
    blank = jnp.zeros((3, GW, GW), jnp.bfloat16)

    greeted = jnp.where(has_below, 1, 0) + jnp.where(is_top, 0, 1) + (shards - 1)
    column = lax.rem(lax.broadcasted_iota(jnp.int32, (rows, GW), 0), width)
    at_left = column == 0
    at_right = column == width - 1
    chunk = GW if rows % GW == 0 and GW % width == 0 else rows
    lane_column = lax.rem(lax.broadcasted_iota(jnp.int32, (GW, chunk), 1), width)
    lane_left = lane_column == 0
    lane_right = lane_column == width - 1

    def put(slot, field):
        wide = field.astype(jnp.float32)
        ahead = jnp.where(at_right, 0.0, pltpu.roll(wide, rows - 1, 0)).astype(jnp.bfloat16)
        for place, piece in enumerate((field, ahead)):
            padded[slot, place, :, width : width + cells, :] = piece.reshape(images, cells, GW)

    def slab(slot, places, order):
        return jnp.concatenate(
            [
                padded[slot, place, :, row * width : row * width + cells, :].reshape(rows, GW)
                for place in places
                for row in order
            ],
            axis=1,
        )

    def mix(slot, kernel):
        wide = lax.dot_general(
            slab(slot, (0, 1), (0, 1, 2)),
            kernel.reshape(6 * GW, 2 * GW),
            (((1,), (0,)), ((), ())),
            preferred_element_type=jnp.float32,
        )
        return wide[:, GW:] + jnp.where(at_left, 0.0, pltpu.roll(wide[:, :GW], 1, 0))

    def turned(field):
        flat = field.T
        parts = ([], [], [])
        for start in range(0, rows, chunk):
            piece = flat[:, start : start + chunk].astype(jnp.float32)
            left = jnp.where(lane_left, 0.0, pltpu.roll(piece, 1, 1))
            right = jnp.where(lane_right, 0.0, pltpu.roll(piece, chunk - 1, 1))
            parts[0].append(left.astype(jnp.bfloat16))
            parts[1].append(flat[:, start : start + chunk])
            parts[2].append(right.astype(jnp.bfloat16))
        return jnp.concatenate([jnp.concatenate(part, axis=1) for part in parts], axis=0)

    def term_of(field, slot):
        return lax.dot_general(
            turned(field),
            slab(slot, (0,), (2, 1, 0)),
            (((1,), (0,)), ((), ())),
            preferred_element_type=jnp.float32,
        )

    def hand_on(branch, group, field, slot):
        term = term_of(field, slot)
        for k in range(9):
            down, side = divmod(k, 3)
            here = (
                slice(side * GW, (side + 1) * GW),
                slice(down * GW, (down + 1) * GW),
            )
            block = (acc[(branch, group, *here)] + term[here]) * (1.0 / cells)
            gown[branch, group, k * GW : (k + 1) * GW, :] = block
            gsend[branch, group, k * GW : (k + 1) * GW, :] = block.astype(jnp.bfloat16)
        waiting = branch == 0 and shards > 1

        @pl.when(jnp.logical_or(not waiting, jnp.logical_or(lax.rem(me, 2) == 0, group < groups - 1)))
        def _():
            for offset in range(1, shards):
                share_copy(group, branch, offset).start()

    def prepare(branch, group):
        weights[branch, group, 3:6, :, 0:GW] = blank
        flipped[branch, group, 3:6, :, 0:GW] = blank
        for down in range(3):
            for side, (row, place) in enumerate(((0, 0), (0, 1), (3, 1))):
                from_row, from_place = ((0, 0), (0, 1), (3, 1))[2 - side]
                flipped[branch, group, row + down, :, place * GW : (place + 1) * GW] = weights[
                    branch, group, from_row + 2 - down, :, from_place * GW : (from_place + 1) * GW
                ].T

    def section(step, tick, group, first, last):
        def give(*copies):
            @pl.when(has_below)
            def _():
                for copy in copies:
                    below_copy(tick, group, *copy).start()

        def keep(stream, value):
            if last:
                final_ref[stream, :, lanes(group)] = value
            else:
                outbuf[tick, group, stream] = value

        def stream(at):
            return inbuf[tick, group, at].astype(jnp.float32)

        if first:
            first_copy(group).wait()
            weights_arrived(group, 1)
        else:
            arrived(tick, group, 0)
        one = stream(0)
        act_one = jax.nn.silu(one).astype(jnp.bfloat16)
        put(0, act_one)
        put(1, inbuf[tick, group, 3])
        if last:
            hand_on(1, group, act_one, 1)
        mixed_one = mix(0, weights[1, group])
        if first:
            input_two = (stream(1) - mixed_one).astype(jnp.bfloat16)
            keep(1, input_two)

            @pl.when(step == 0)
            def _():
                pl.semaphore_wait(barrier, greeted)

            give((1, 1, 1))
            prepare(1, group)
        mixed_two = mix(1, flipped[1, group]) * smooth_grad(one)
        if not first:
            arrived(tick, group, 1)
            input_two = (stream(1) - mixed_one).astype(jnp.bfloat16)
            keep(1, input_two)
        total_one = (stream(2) + mixed_two).astype(jnp.bfloat16)
        keep(2, total_one)
        if first:
            give((2, 1, 1))
            weights_arrived(group, 0)
            prepare(0, group)
        wide_two = input_two.astype(jnp.float32)
        act_two = jax.nn.silu(wide_two).astype(jnp.bfloat16)
        put(2, act_two)
        put(3, total_one)
        if last:
            hand_on(0, group, act_two, 3)
        keep(0, (stream(0) - mix(2, weights[0, group])).astype(jnp.bfloat16))
        keep(
            3,
            (stream(3) + mix(3, flipped[0, group]) * smooth_grad(wide_two)).astype(jnp.bfloat16),
        )
        if first:
            give((0, 1, 0), (3, 1, 0))
            acc[1, group] = term_of(act_one, 1)
            acc[0, group] = term_of(act_two, 3)
        elif not last:
            give((0, 1, 0), (3, 1, 0), (1, 2, 1))
            acc[1, group] += term_of(act_one, 1)
            acc[0, group] += term_of(act_two, 3)

    @pl.loop(0, ticks * groups)
    def _(step):
        word = jnp.int32(0)
        for place in range(0, len(order), 3):
            packed = 0
            for at, (at_group, at_tick) in enumerate(order[place : place + 3]):
                packed |= (at_group * 32 + at_tick) << (10 * at)
            word = jnp.where(step >= place, packed, word)
        entry = lax.shift_right_logical(word, 10 * lax.rem(step, 3))
        tick = entry & 31
        group = lax.shift_right_logical(entry, 5) & 31

        @pl.when(tick == 0)
        def _():
            section(step, 0, group, True, False)

        @pl.when(jnp.logical_and(tick > 0, tick < ticks - 1))
        def _():
            section(step, tick, group, False, False)

        @pl.when(tick == ticks - 1)
        def _():
            section(step, ticks - 1, group, False, True)

    def shared(branch):
        for offset in range(1, shards):
            every = gsend.at[branch, :, pl.ds(0, share)]
            pltpu.make_async_copy(every, every, gsend_sem.at[offset - 1, branch]).wait()

    if shards > 1:

        @pl.when(upper)
        def _():
            pl.semaphore_wait(turn_sem, 1)
            for offset in range(1, shards):
                share_copy(groups - 1, 0, offset).start()

        shared(1)

        @pl.when(lower)
        def _():
            pl.semaphore_signal(turn_sem, inc=1, device_id={"section": me + 1}, device_id_type=MESH)

    @pl.loop(0, groups)
    def _(group):
        for branch in (1, 0):
            total = gown[branch, group, pl.ds(pl.multiple_of(mine * share, 16), share), :]
            for offset in range(1, shards):
                share_copy(group, branch, offset).wait_recv()
                total = total + grecv[offset - 1, branch, group].astype(jnp.float32)
            grads_ref[branch, :, lanes(group)] = total

    shared(0)

    @pl.when(has_below)
    def _():
        for part in range(2):
            every = outbuf.at[pl.ds(0, ticks - 1), :, pl.ds(0, 2)]
            pltpu.make_async_copy(every, every, send_sem.at[part]).wait()


def write_kernel(final_ref, grads_ref, final_out, grads_out, sems):
    copies = [
        pltpu.make_async_copy(grads_ref, grads_out, sems.at[0]),
        pltpu.make_async_copy(final_ref, final_out, sems.at[1]),
    ]
    for copy in copies:
        copy.start()
    for copy in copies:
        copy.wait()


def on_device(section_states, conv_kernels, top_feed):
    _, _, images, height, width, chans = section_states.shape
    ticks = top_feed.shape[0] + 1
    groups = chans // GW
    shards = lax.axis_size("dp")
    taps_rows = conv_kernels.shape[2]
    share = taps_rows // shards
    rows = images * height * width
    states = section_states.reshape(4, rows, chans)
    feed = top_feed.reshape(ticks - 1, 4, rows, chans)
    dims = (ticks, groups, images, height, width, share, shards)
    anywhere = pl.BlockSpec(memory_space=pltpu.HBM)
    dma = pltpu.SemaphoreType.DMA
    final, grads = pl.pallas_call(
        functools.partial(fused_kernel, dims),
        out_shape=(
            pltpu.VMEM((4, rows, chans), jnp.bfloat16),
            pltpu.VMEM((2, share, chans), jnp.float32),
        ),
        in_specs=[anywhere] * 3,
        out_specs=[pl.BlockSpec(memory_space=pltpu.VMEM)] * 2,
        scratch_shapes=[
            pltpu.VMEM((ticks, groups, 4, rows, GW), jnp.bfloat16),
            pltpu.VMEM((ticks, groups, 4, rows, GW), jnp.bfloat16),
            pltpu.VMEM((2, groups, 6, GW, 2 * GW), jnp.bfloat16),
            pltpu.VMEM((2, groups, 6, GW, 2 * GW), jnp.bfloat16),
            pltpu.VMEM((4, 2, images, (height + 2) * width, GW), jnp.bfloat16),
            pltpu.VMEM((2, groups, 3 * GW, 3 * GW), jnp.float32),
            pltpu.VMEM((2, groups, taps_rows, GW), jnp.bfloat16),
            pltpu.VMEM((2, groups, taps_rows, GW), jnp.float32),
            pltpu.VMEM((max(shards - 1, 1), 2, groups, share, GW), jnp.bfloat16),
            dma((ticks, groups, 2)),
            dma((2,)),
            dma((2, groups)),
            pltpu.SemaphoreType.REGULAR,
            dma((max(shards - 1, 1), 2)),
            dma((max(shards - 1, 1), 2, groups)),
        ],
        compiler_params=pltpu.CompilerParams(
            collective_id=0, has_side_effects=True, vmem_limit_bytes=56 * 1024 * 1024
        ),
    )(states, conv_kernels.reshape(2, 3, 3, GW, chans), feed)
    final, grads = pl.pallas_call(
        write_kernel,
        out_shape=(
            jax.ShapeDtypeStruct(final.shape, final.dtype),
            jax.ShapeDtypeStruct(grads.shape, grads.dtype),
        ),
        in_specs=[pl.BlockSpec(memory_space=pltpu.VMEM)] * 2,
        out_specs=[anywhere] * 2,
        scratch_shapes=[dma((2,))],
        compiler_params=pltpu.CompilerParams(vmem_limit_bytes=1024 * 1024),
    )(final, grads)
    return (
        final.reshape(section_states.shape),
        grads.reshape(1, 2, share, chans),
    )


def solution(mesh):
    return jax.shard_map(
        on_device,
        mesh=mesh,
        in_specs=(
            P("section", None, "dp", None, None, None),
            P("section", None, None, None),
            P(None, None, "dp", None, None, None),
        ),
        out_specs=(P("section", None, "dp", None, None, None), P("section", None, "dp", None)),
        check_vma=False,
    )
```

```python
import functools

import jax
import jax.numpy as jnp
from jax import lax
from jax.experimental import pallas as pl
from jax.experimental.pallas import tpu as pltpu
from jax.sharding import PartitionSpec as P

GW = 128
MESH = pl.DeviceIdType.MESH
PARTS = ((0, 1, 0), (3, 1, 0), (1, 2, 1))


def smooth_grad(value):
    sigma = jax.nn.sigmoid(value)
    return sigma * (1.0 + value * (1.0 - sigma))


def steps_in_order(groups, ticks):
    tuned = ((0, 0), (0, 1), (1, 0), (0, 2), (1, 1), (0, 3), (2, 0), (1, 2), (2, 1), (1, 3), (3, 0), (2, 2), (3, 1), (2, 3), (3, 2), (3, 3))
    if sorted(tuned) == [(group, tick) for group in range(groups) for tick in range(ticks)]:
        return tuned
    return [(group, tick) for tick in range(ticks) for group in range(groups)]


def fused_kernel(
    dims,
    states_ref,
    kernels_ref,
    feed_ref,
    final_ref,
    grads_ref,
    inbuf,
    outbuf,
    weights,
    flipped,
    padded,
    acc,
    gsend,
    gown,
    grecv,
    first_sem,
    in_sem,
    send_sem,
    weight_sem,
    turn_sem,
    gsend_sem,
    grecv_sem,
):
    ticks, groups, images, height, width, share, shards = dims
    cells = height * width
    order = steps_in_order(groups, ticks)
    rows = images * cells
    pad = (height + 2) * width
    me = lax.axis_index("section")
    count = lax.axis_size("section")
    mine = lax.axis_index("dp")
    is_top = me == count - 1
    lower = jnp.logical_and(lax.rem(me, 2) == 0, me < count - 1)
    upper = lax.rem(me, 2) == 1
    has_below = me > 0

    def lanes(group):
        start = group * GW
        return pl.ds(start if isinstance(group, int) else pl.multiple_of(start, GW), GW)

    def first_copy(group):
        return pltpu.make_async_copy(
            states_ref.at[:, :, lanes(group)], inbuf.at[0, group], first_sem.at[group]
        )

    def feed_copies(tick, group):
        for first, size, part in PARTS:
            yield pltpu.make_async_copy(
                feed_ref.at[tick - 1, pl.ds(first, size), :, lanes(group)],
                inbuf.at[tick, group, pl.ds(first, size)],
                in_sem.at[tick - 1, group, part],
            )

    def weight_copy(group, branch, column):
        row, place = ((0, 0), (0, 1), (3, 1))[column]
        return pltpu.make_async_copy(
            kernels_ref.at[branch, :, column, :, lanes(group)],
            weights.at[branch, group, pl.ds(row, 3), :, pl.ds(place * GW, GW)],
            weight_sem.at[group],
        )

    def weights_arrived(group):
        whole = kernels_ref.at[:, :, :, :, lanes(group)]
        pltpu.make_async_copy(whole, whole, weight_sem.at[group]).wait()

    def below_copy(tick, group, first, size, part):
        return pltpu.make_async_remote_copy(
            src_ref=outbuf.at[tick, group, pl.ds(first, size)],
            dst_ref=inbuf.at[tick + 1, group, pl.ds(first, size)],
            send_sem=send_sem.at[0],
            recv_sem=in_sem.at[tick, group, part],
            device_id={"section": me - 1},
            device_id_type=MESH,
        )

    def arrived(tick, group, part):
        pair = inbuf.at[tick, group, pl.ds(1, 2)]
        pltpu.make_async_copy(pair, pair, in_sem.at[tick - 1, group, part]).wait()

    def share_copy(group, branch, offset):
        partner = lax.rem(mine + offset, shards)
        return pltpu.make_async_remote_copy(
            src_ref=gsend.at[branch, group, pl.ds(pl.multiple_of(partner * share, 16), share)],
            dst_ref=grecv.at[offset - 1, branch, group],
            send_sem=gsend_sem.at[offset - 1, branch],
            recv_sem=grecv_sem.at[offset - 1, group],
            device_id={"dp": partner},
            device_id_type=MESH,
        )

    barrier = pltpu.get_barrier_semaphore()

    @pl.when(has_below)
    def _():
        pl.semaphore_signal(barrier, inc=1, device_id={"section": me - 1}, device_id_type=MESH)

    @pl.when(jnp.logical_not(is_top))
    def _():
        pl.semaphore_signal(barrier, inc=1, device_id={"section": me + 1}, device_id_type=MESH)

    for offset in range(1, shards):
        pl.semaphore_signal(
            barrier,
            inc=1,
            device_id={"dp": lax.rem(mine + offset, shards)},
            device_id_type=MESH,
        )

    for group in range(groups):
        first_copy(group).start()
        for branch in (1, 0):
            for column in range(3):
                weight_copy(group, branch, column).start()

    @pl.when(is_top)
    def _():
        @pl.loop(1, ticks)
        def _(tick):
            for group in range(groups):
                for copy in feed_copies(tick, group):
                    copy.start()

    edge = jnp.zeros((4, 2, images, width, GW), jnp.bfloat16)
    padded[:, :, :, 0:width, :] = edge
    padded[:, :, :, pad - width : pad, :] = edge
    blank = jnp.zeros((3, GW, GW), jnp.bfloat16)

    greeted = jnp.where(has_below, 1, 0) + jnp.where(is_top, 0, 1) + (shards - 1)
    column = lax.rem(lax.broadcasted_iota(jnp.int32, (rows, GW), 0), width)
    at_left = column == 0
    at_right = column == width - 1
    chunk = GW if rows % GW == 0 and GW % width == 0 else rows
    lane_column = lax.rem(lax.broadcasted_iota(jnp.int32, (GW, chunk), 1), width)
    lane_left = lane_column == 0
    lane_right = lane_column == width - 1

    def put(slot, field):
        wide = field.astype(jnp.float32)
        ahead = jnp.where(at_right, 0.0, pltpu.roll(wide, rows - 1, 0)).astype(jnp.bfloat16)
        for place, piece in enumerate((field, ahead)):
            padded[slot, place, :, width : width + cells, :] = piece.reshape(images, cells, GW)

    def slab(slot, places, order):
        return jnp.concatenate(
            [
                padded[slot, place, :, row * width : row * width + cells, :].reshape(rows, GW)
                for place in places
                for row in order
            ],
            axis=1,
        )

    def mix(slot, kernel):
        wide = lax.dot_general(
            slab(slot, (0, 1), (0, 1, 2)),
            kernel.reshape(6 * GW, 2 * GW),
            (((1,), (0,)), ((), ())),
            preferred_element_type=jnp.float32,
        )
        return wide[:, GW:] + jnp.where(at_left, 0.0, pltpu.roll(wide[:, :GW], 1, 0))

    def turned(field):
        flat = field.T
        parts = ([], [], [])
        for start in range(0, rows, chunk):
            piece = flat[:, start : start + chunk].astype(jnp.float32)
            left = jnp.where(lane_left, 0.0, pltpu.roll(piece, 1, 1))
            right = jnp.where(lane_right, 0.0, pltpu.roll(piece, chunk - 1, 1))
            parts[0].append(left.astype(jnp.bfloat16))
            parts[1].append(flat[:, start : start + chunk])
            parts[2].append(right.astype(jnp.bfloat16))
        return jnp.concatenate([jnp.concatenate(part, axis=1) for part in parts], axis=0)

    def term_of(field, slot):
        return lax.dot_general(
            turned(field),
            slab(slot, (0,), (2, 1, 0)),
            (((1,), (0,)), ((), ())),
            preferred_element_type=jnp.float32,
        )

    def hand_on(branch, group, field, slot):
        term = term_of(field, slot)
        for k in range(9):
            down, side = divmod(k, 3)
            here = (
                slice(side * GW, (side + 1) * GW),
                slice(down * GW, (down + 1) * GW),
            )
            block = (acc[(branch, group, *here)] + term[here]) * (1.0 / cells)
            gown[branch, group, k * GW : (k + 1) * GW, :] = block
            gsend[branch, group, k * GW : (k + 1) * GW, :] = block.astype(jnp.bfloat16)
        waiting = branch == 0 and shards > 1

        @pl.when(jnp.logical_or(not waiting, jnp.logical_or(lax.rem(me, 2) == 0, group < groups - 1)))
        def _():
            for offset in range(1, shards):
                share_copy(group, branch, offset).start()

    def prepare(branch, group):
        weights[branch, group, 3:6, :, 0:GW] = blank
        flipped[branch, group, 3:6, :, 0:GW] = blank
        for down in range(3):
            for side, (row, place) in enumerate(((0, 0), (0, 1), (3, 1))):
                from_row, from_place = ((0, 0), (0, 1), (3, 1))[2 - side]
                flipped[branch, group, row + down, :, place * GW : (place + 1) * GW] = weights[
                    branch, group, from_row + 2 - down, :, from_place * GW : (from_place + 1) * GW
                ].T

    def section(step, tick, group, first, last):
        def give(*copies):
            @pl.when(has_below)
            def _():
                for copy in copies:
                    below_copy(tick, group, *copy).start()

        def keep(stream, value):
            if last:
                final_ref[stream, :, lanes(group)] = value
            else:
                outbuf[tick, group, stream] = value

        def stream(at):
            return inbuf[tick, group, at].astype(jnp.float32)

        if first:
            first_copy(group).wait()
            weights_arrived(group)
        else:
            arrived(tick, group, 0)
        one = stream(0)
        act_one = jax.nn.silu(one).astype(jnp.bfloat16)
        put(0, act_one)
        put(1, inbuf[tick, group, 3])
        if last:
            hand_on(1, group, act_one, 1)
        mixed_one = mix(0, weights[1, group])
        if first:
            input_two = (stream(1) - mixed_one).astype(jnp.bfloat16)
            keep(1, input_two)

            @pl.when(step == 0)
            def _():
                pl.semaphore_wait(barrier, greeted)

            give((1, 1, 1))
            prepare(1, group)
        mixed_two = mix(1, flipped[1, group]) * smooth_grad(one)
        if not first:
            arrived(tick, group, 1)
            input_two = (stream(1) - mixed_one).astype(jnp.bfloat16)
            keep(1, input_two)
        total_one = (stream(2) + mixed_two).astype(jnp.bfloat16)
        keep(2, total_one)
        if first:
            give((2, 1, 1))
            prepare(0, group)
        wide_two = input_two.astype(jnp.float32)
        act_two = jax.nn.silu(wide_two).astype(jnp.bfloat16)
        put(2, act_two)
        put(3, total_one)
        if last:
            hand_on(0, group, act_two, 3)
        keep(0, (stream(0) - mix(2, weights[0, group])).astype(jnp.bfloat16))
        keep(
            3,
            (stream(3) + mix(3, flipped[0, group]) * smooth_grad(wide_two)).astype(jnp.bfloat16),
        )
        if first:
            give((0, 1, 0), (3, 1, 0))
            acc[1, group] = term_of(act_one, 1)
            acc[0, group] = term_of(act_two, 3)
        elif not last:
            give((0, 1, 0), (3, 1, 0), (1, 2, 1))
            acc[1, group] += term_of(act_one, 1)
            acc[0, group] += term_of(act_two, 3)

    @pl.loop(0, ticks * groups)
    def _(step):
        word = jnp.int32(0)
        for place in range(0, len(order), 3):
            packed = 0
            for at, (at_group, at_tick) in enumerate(order[place : place + 3]):
                packed |= (at_group * 32 + at_tick) << (10 * at)
            word = jnp.where(step >= place, packed, word)
        entry = lax.shift_right_logical(word, 10 * lax.rem(step, 3))
        tick = entry & 31
        group = lax.shift_right_logical(entry, 5) & 31

        @pl.when(tick == 0)
        def _():
            section(step, 0, group, True, False)

        @pl.when(jnp.logical_and(tick > 0, tick < ticks - 1))
        def _():
            section(step, tick, group, False, False)

        @pl.when(tick == ticks - 1)
        def _():
            section(step, ticks - 1, group, False, True)

    def shared(branch):
        for offset in range(1, shards):
            every = gsend.at[branch, :, pl.ds(0, share)]
            pltpu.make_async_copy(every, every, gsend_sem.at[offset - 1, branch]).wait()

    if shards > 1:

        @pl.when(upper)
        def _():
            pl.semaphore_wait(turn_sem, 1)
            for offset in range(1, shards):
                share_copy(groups - 1, 0, offset).start()

        shared(1)

        @pl.when(lower)
        def _():
            pl.semaphore_signal(turn_sem, inc=1, device_id={"section": me + 1}, device_id_type=MESH)

    @pl.loop(0, groups)
    def _(group):
        for offset in range(1, shards):
            both = grecv.at[offset - 1, :, group]
            pltpu.make_async_copy(both, both, grecv_sem.at[offset - 1, group]).wait()
        for branch in (1, 0):
            total = gown[branch, group, pl.ds(pl.multiple_of(mine * share, 16), share), :]
            for offset in range(1, shards):
                total = total + grecv[offset - 1, branch, group].astype(jnp.float32)
            grads_ref[branch, :, lanes(group)] = total

    shared(0)

    @pl.when(has_below)
    def _():
        every = outbuf.at[pl.ds(0, ticks - 1)]
        pltpu.make_async_copy(every, every, send_sem.at[0]).wait()


def write_kernel(final_ref, grads_ref, final_out, grads_out, sems):
    copies = [
        pltpu.make_async_copy(grads_ref, grads_out, sems.at[0]),
        pltpu.make_async_copy(final_ref, final_out, sems.at[1]),
    ]
    for copy in copies:
        copy.start()
    for copy in copies:
        copy.wait()


def on_device(section_states, conv_kernels, top_feed):
    _, _, images, height, width, chans = section_states.shape
    ticks = top_feed.shape[0] + 1
    groups = chans // GW
    shards = lax.axis_size("dp")
    taps_rows = conv_kernels.shape[2]
    share = taps_rows // shards
    rows = images * height * width
    states = section_states.reshape(4, rows, chans)
    feed = top_feed.reshape(ticks - 1, 4, rows, chans)
    dims = (ticks, groups, images, height, width, share, shards)
    anywhere = pl.BlockSpec(memory_space=pltpu.HBM)
    dma = pltpu.SemaphoreType.DMA
    final, grads = pl.pallas_call(
        functools.partial(fused_kernel, dims),
        out_shape=(
            pltpu.VMEM((4, rows, chans), jnp.bfloat16),
            pltpu.VMEM((2, share, chans), jnp.float32),
        ),
        in_specs=[anywhere] * 3,
        out_specs=[pl.BlockSpec(memory_space=pltpu.VMEM)] * 2,
        scratch_shapes=[
            pltpu.VMEM((ticks, groups, 4, rows, GW), jnp.bfloat16),
            pltpu.VMEM((ticks, groups, 4, rows, GW), jnp.bfloat16),
            pltpu.VMEM((2, groups, 6, GW, 2 * GW), jnp.bfloat16),
            pltpu.VMEM((2, groups, 6, GW, 2 * GW), jnp.bfloat16),
            pltpu.VMEM((4, 2, images, (height + 2) * width, GW), jnp.bfloat16),
            pltpu.VMEM((2, groups, 3 * GW, 3 * GW), jnp.float32),
            pltpu.VMEM((2, groups, taps_rows, GW), jnp.bfloat16),
            pltpu.VMEM((2, groups, taps_rows, GW), jnp.float32),
            pltpu.VMEM((max(shards - 1, 1), 2, groups, share, GW), jnp.bfloat16),
            dma((groups,)),
            dma((ticks - 1, groups, 2)),
            dma((1,)),
            dma((groups,)),
            pltpu.SemaphoreType.REGULAR,
            dma((max(shards - 1, 1), 2)),
            dma((max(shards - 1, 1), groups)),
        ],
        compiler_params=pltpu.CompilerParams(
            collective_id=0, has_side_effects=True, vmem_limit_bytes=56 * 1024 * 1024
        ),
    )(states, conv_kernels.reshape(2, 3, 3, GW, chans), feed)
    final, grads = pl.pallas_call(
        write_kernel,
        out_shape=(
            jax.ShapeDtypeStruct(final.shape, final.dtype),
            jax.ShapeDtypeStruct(grads.shape, grads.dtype),
        ),
        in_specs=[pl.BlockSpec(memory_space=pltpu.VMEM)] * 2,
        out_specs=[anywhere] * 2,
        scratch_shapes=[dma((2,))],
        compiler_params=pltpu.CompilerParams(vmem_limit_bytes=1024 * 1024),
    )(final, grads)
    return (
        final.reshape(section_states.shape),
        grads.reshape(1, 2, share, chans),
    )


def solution(mesh):
    return jax.shard_map(
        on_device,
        mesh=mesh,
        in_specs=(
            P("section", None, "dp", None, None, None),
            P("section", None, None, None),
            P(None, None, "dp", None, None, None),
        ),
        out_specs=(P("section", None, "dp", None, None, None), P("section", None, "dp", None)),
        check_vma=False,
    )
```

```python
import functools

import jax
import jax.numpy as jnp
from jax import lax
from jax.experimental import pallas as pl
from jax.experimental.pallas import tpu as pltpu
from jax.sharding import PartitionSpec as P

GW = 128
MESH = pl.DeviceIdType.MESH
PARTS = ((0, 1, 0), (3, 1, 0), (1, 2, 1))


def smooth_grad(value):
    sigma = jax.nn.sigmoid(value)
    return sigma * (1.0 + value * (1.0 - sigma))


def steps_in_order(groups, ticks):
    tuned = ((0, 0), (0, 1), (1, 0), (0, 2), (1, 1), (0, 3), (2, 0), (1, 2), (2, 1), (1, 3), (3, 0), (2, 2), (3, 1), (2, 3), (3, 2), (3, 3))
    if sorted(tuned) == [(group, tick) for group in range(groups) for tick in range(ticks)]:
        return tuned
    return [(group, tick) for tick in range(ticks) for group in range(groups)]


def fused_kernel(
    dims,
    states_ref,
    kernels_ref,
    feed_ref,
    final_ref,
    grads_ref,
    inbuf,
    outbuf,
    weights,
    flipped,
    padded,
    acc,
    gsend,
    gown,
    grecv,
    first_sem,
    in_sem,
    send_sem,
    weight_sem,
    turn_sem,
    gsend_sem,
    grecv_sem,
):
    ticks, groups, images, height, width, share, shards = dims
    cells = height * width
    order = steps_in_order(groups, ticks)
    rows = images * cells
    pad = (height + 2) * width
    me = lax.axis_index("section")
    count = lax.axis_size("section")
    mine = lax.axis_index("dp")
    is_top = me == count - 1
    lower = jnp.logical_and(lax.rem(me, 2) == 0, me < count - 1)
    upper = lax.rem(me, 2) == 1
    has_below = me > 0

    def lanes(group):
        start = group * GW
        return pl.ds(start if isinstance(group, int) else pl.multiple_of(start, GW), GW)

    def first_copy(group):
        return pltpu.make_async_copy(
            states_ref.at[:, :, lanes(group)], inbuf.at[0, group], first_sem.at[group]
        )

    def feed_copies(tick, group):
        for first, size, part in PARTS:
            yield pltpu.make_async_copy(
                feed_ref.at[tick - 1, pl.ds(first, size), :, lanes(group)],
                inbuf.at[tick, group, pl.ds(first, size)],
                in_sem.at[tick - 1, group, part],
            )

    def weight_copy(group, branch, column):
        row, place = ((0, 0), (0, 1), (3, 1))[column]
        return pltpu.make_async_copy(
            kernels_ref.at[branch, :, column, :, lanes(group)],
            weights.at[branch, group, pl.ds(row, 3), :, pl.ds(place * GW, GW)],
            weight_sem.at[group],
        )

    def weights_arrived(group):
        whole = kernels_ref.at[:, :, :, :, lanes(group)]
        pltpu.make_async_copy(whole, whole, weight_sem.at[group]).wait()

    def below_copy(tick, group, first, size, part):
        return pltpu.make_async_remote_copy(
            src_ref=outbuf.at[tick, group, pl.ds(first, size)],
            dst_ref=inbuf.at[tick + 1, group, pl.ds(first, size)],
            send_sem=send_sem.at[0],
            recv_sem=in_sem.at[tick, group, part],
            device_id={"section": me - 1},
            device_id_type=MESH,
        )

    def arrived(tick, group, part):
        pair = inbuf.at[tick, group, pl.ds(1, 2)]
        pltpu.make_async_copy(pair, pair, in_sem.at[tick - 1, group, part]).wait()

    def share_copy(group, branch, offset):
        partner = lax.rem(mine + offset, shards)
        return pltpu.make_async_remote_copy(
            src_ref=gsend.at[branch, group, pl.ds(pl.multiple_of(partner * share, 16), share)],
            dst_ref=grecv.at[offset - 1, branch, group],
            send_sem=gsend_sem.at[offset - 1, branch],
            recv_sem=grecv_sem.at[offset - 1, group],
            device_id={"dp": partner},
            device_id_type=MESH,
        )

    barrier = pltpu.get_barrier_semaphore()

    @pl.when(has_below)
    def _():
        pl.semaphore_signal(barrier, inc=1, device_id={"section": me - 1}, device_id_type=MESH)

    @pl.when(jnp.logical_not(is_top))
    def _():
        pl.semaphore_signal(barrier, inc=1, device_id={"section": me + 1}, device_id_type=MESH)

    for offset in range(1, shards):
        pl.semaphore_signal(
            barrier,
            inc=1,
            device_id={"dp": lax.rem(mine + offset, shards)},
            device_id_type=MESH,
        )

    for group in range(groups):
        first_copy(group).start()
        for branch in (1, 0):
            for column in range(3):
                weight_copy(group, branch, column).start()

    @pl.when(is_top)
    def _():
        @pl.loop(1, ticks)
        def _(tick):
            for group in range(groups):
                for copy in feed_copies(tick, group):
                    copy.start()

    edge = jnp.zeros((4, 2, images, width, GW), jnp.bfloat16)
    padded[:, :, :, 0:width, :] = edge
    padded[:, :, :, pad - width : pad, :] = edge
    blank = jnp.zeros((3, GW, GW), jnp.bfloat16)

    greeted = jnp.where(has_below, 1, 0) + jnp.where(is_top, 0, 1) + (shards - 1)
    column = lax.rem(lax.broadcasted_iota(jnp.int32, (rows, GW), 0), width)
    at_left = column == 0
    at_right = column == width - 1
    chunk = GW if rows % GW == 0 and GW % width == 0 else rows
    lane_column = lax.rem(lax.broadcasted_iota(jnp.int32, (GW, chunk), 1), width)
    lane_left = lane_column == 0
    lane_right = lane_column == width - 1

    def put(slot, field):
        wide = field.astype(jnp.float32)
        ahead = jnp.where(at_right, 0.0, pltpu.roll(wide, rows - 1, 0)).astype(jnp.bfloat16)
        for place, piece in enumerate((field, ahead)):
            padded[slot, place, :, width : width + cells, :] = piece.reshape(images, cells, GW)

    def slab(slot, places, order):
        return jnp.concatenate(
            [
                padded[slot, place, :, row * width : row * width + cells, :].reshape(rows, GW)
                for place in places
                for row in order
            ],
            axis=1,
        )

    def mix(slot, kernel):
        wide = lax.dot_general(
            slab(slot, (0, 1), (0, 1, 2)),
            kernel.reshape(6 * GW, 2 * GW),
            (((1,), (0,)), ((), ())),
            preferred_element_type=jnp.float32,
        )
        return wide[:, GW:] + jnp.where(at_left, 0.0, pltpu.roll(wide[:, :GW], 1, 0))

    def turned(field):
        flat = field.T
        parts = ([], [], [])
        for start in range(0, rows, chunk):
            piece = flat[:, start : start + chunk].astype(jnp.float32)
            left = jnp.where(lane_left, 0.0, pltpu.roll(piece, 1, 1))
            right = jnp.where(lane_right, 0.0, pltpu.roll(piece, chunk - 1, 1))
            parts[0].append(left.astype(jnp.bfloat16))
            parts[1].append(flat[:, start : start + chunk])
            parts[2].append(right.astype(jnp.bfloat16))
        return jnp.concatenate([jnp.concatenate(part, axis=1) for part in parts], axis=0)

    def term_of(field, slot):
        return lax.dot_general(
            turned(field),
            slab(slot, (0,), (2, 1, 0)),
            (((1,), (0,)), ((), ())),
            preferred_element_type=jnp.float32,
        )

    def hand_on(branch, group, field, slot):
        term = term_of(field, slot)
        for k in range(9):
            down, side = divmod(k, 3)
            here = (
                slice(side * GW, (side + 1) * GW),
                slice(down * GW, (down + 1) * GW),
            )
            block = (acc[(branch, group, *here)] + term[here]) * (1.0 / cells)
            gown[branch, group, k * GW : (k + 1) * GW, :] = block
            gsend[branch, group, k * GW : (k + 1) * GW, :] = block.astype(jnp.bfloat16)
        waiting = branch == 0 and shards > 1

        @pl.when(jnp.logical_or(not waiting, jnp.logical_or(lax.rem(me, 2) == 0, group < groups - 1)))
        def _():
            for offset in range(1, shards):
                share_copy(group, branch, offset).start()

    def prepare(branch, group):
        weights[branch, group, 3:6, :, 0:GW] = blank
        flipped[branch, group, 3:6, :, 0:GW] = blank
        for down in range(3):
            for side, (row, place) in enumerate(((0, 0), (0, 1), (3, 1))):
                from_row, from_place = ((0, 0), (0, 1), (3, 1))[2 - side]
                flipped[branch, group, row + down, :, place * GW : (place + 1) * GW] = weights[
                    branch, group, from_row + 2 - down, :, from_place * GW : (from_place + 1) * GW
                ].T

    def section(step, tick, group, first, last):
        def give(*copies):
            @pl.when(has_below)
            def _():
                for copy in copies:
                    below_copy(tick, group, *copy).start()

        def keep(stream, value):
            if last:
                final_ref[stream, :, lanes(group)] = value
            else:
                outbuf[tick, group, stream] = value

        def stream(at):
            return inbuf[tick, group, at].astype(jnp.float32)

        if first:
            first_copy(group).wait()
            weights_arrived(group)
        else:
            arrived(tick, group, 0)
        one = stream(0)
        act_one = jax.nn.silu(one).astype(jnp.bfloat16)
        put(0, act_one)
        put(1, inbuf[tick, group, 3])
        if last:
            hand_on(1, group, act_one, 1)
        mixed_one = mix(0, weights[1, group])
        if first:
            input_two = (stream(1) - mixed_one).astype(jnp.bfloat16)
            keep(1, input_two)

            @pl.when(step == 0)
            def _():
                pl.semaphore_wait(barrier, greeted)

            give((1, 1, 1))
            prepare(1, group)
        mixed_two = mix(1, flipped[1, group]) * smooth_grad(one)
        if not first:
            arrived(tick, group, 1)
            input_two = (stream(1) - mixed_one).astype(jnp.bfloat16)
            keep(1, input_two)
        total_one = (stream(2) + mixed_two).astype(jnp.bfloat16)
        keep(2, total_one)
        if first:
            give((2, 1, 1))
            prepare(0, group)
        wide_two = input_two.astype(jnp.float32)
        act_two = jax.nn.silu(wide_two).astype(jnp.bfloat16)
        put(2, act_two)
        put(3, total_one)
        if last:
            hand_on(0, group, act_two, 3)
        keep(0, (stream(0) - mix(2, weights[0, group])).astype(jnp.bfloat16))
        if not last:
            give((0, 1, 0))
        keep(
            3,
            (stream(3) + mix(3, flipped[0, group]) * smooth_grad(wide_two)).astype(jnp.bfloat16),
        )
        if first:
            give((3, 1, 0))
            acc[1, group] = term_of(act_one, 1)
            acc[0, group] = term_of(act_two, 3)
        elif not last:
            give((3, 1, 0), (1, 2, 1))
            acc[1, group] += term_of(act_one, 1)
            acc[0, group] += term_of(act_two, 3)

    @pl.loop(0, ticks * groups)
    def _(step):
        word = jnp.int32(0)
        for place in range(0, len(order), 3):
            packed = 0
            for at, (at_group, at_tick) in enumerate(order[place : place + 3]):
                packed |= (at_group * 32 + at_tick) << (10 * at)
            word = jnp.where(step >= place, packed, word)
        entry = lax.shift_right_logical(word, 10 * lax.rem(step, 3))
        tick = entry & 31
        group = lax.shift_right_logical(entry, 5) & 31

        @pl.when(tick == 0)
        def _():
            section(step, 0, group, True, False)

        @pl.when(jnp.logical_and(tick > 0, tick < ticks - 1))
        def _():
            section(step, tick, group, False, False)

        @pl.when(tick == ticks - 1)
        def _():
            section(step, ticks - 1, group, False, True)

    def shared(branch):
        for offset in range(1, shards):
            every = gsend.at[branch, :, pl.ds(0, share)]
            pltpu.make_async_copy(every, every, gsend_sem.at[offset - 1, branch]).wait()

    if shards > 1:

        @pl.when(upper)
        def _():
            pl.semaphore_wait(turn_sem, 1)
            for offset in range(1, shards):
                share_copy(groups - 1, 0, offset).start()

        shared(1)

        @pl.when(lower)
        def _():
            pl.semaphore_signal(turn_sem, inc=1, device_id={"section": me + 1}, device_id_type=MESH)

    @pl.loop(0, groups)
    def _(group):
        for offset in range(1, shards):
            both = grecv.at[offset - 1, :, group]
            pltpu.make_async_copy(both, both, grecv_sem.at[offset - 1, group]).wait()
        for branch in (1, 0):
            total = gown[branch, group, pl.ds(pl.multiple_of(mine * share, 16), share), :]
            for offset in range(1, shards):
                total = total + grecv[offset - 1, branch, group].astype(jnp.float32)
            grads_ref[branch, :, lanes(group)] = total

    shared(0)

    @pl.when(has_below)
    def _():
        every = outbuf.at[pl.ds(0, ticks - 1)]
        pltpu.make_async_copy(every, every, send_sem.at[0]).wait()


def write_kernel(final_ref, grads_ref, final_out, grads_out, sems):
    copies = [
        pltpu.make_async_copy(grads_ref, grads_out, sems.at[0]),
        pltpu.make_async_copy(final_ref, final_out, sems.at[1]),
    ]
    for copy in copies:
        copy.start()
    for copy in copies:
        copy.wait()


def on_device(section_states, conv_kernels, top_feed):
    _, _, images, height, width, chans = section_states.shape
    ticks = top_feed.shape[0] + 1
    groups = chans // GW
    shards = lax.axis_size("dp")
    taps_rows = conv_kernels.shape[2]
    share = taps_rows // shards
    rows = images * height * width
    states = section_states.reshape(4, rows, chans)
    feed = top_feed.reshape(ticks - 1, 4, rows, chans)
    dims = (ticks, groups, images, height, width, share, shards)
    anywhere = pl.BlockSpec(memory_space=pltpu.HBM)
    dma = pltpu.SemaphoreType.DMA
    final, grads = pl.pallas_call(
        functools.partial(fused_kernel, dims),
        out_shape=(
            pltpu.VMEM((4, rows, chans), jnp.bfloat16),
            pltpu.VMEM((2, share, chans), jnp.float32),
        ),
        in_specs=[anywhere] * 3,
        out_specs=[pl.BlockSpec(memory_space=pltpu.VMEM)] * 2,
        scratch_shapes=[
            pltpu.VMEM((ticks, groups, 4, rows, GW), jnp.bfloat16),
            pltpu.VMEM((ticks, groups, 4, rows, GW), jnp.bfloat16),
            pltpu.VMEM((2, groups, 6, GW, 2 * GW), jnp.bfloat16),
            pltpu.VMEM((2, groups, 6, GW, 2 * GW), jnp.bfloat16),
            pltpu.VMEM((4, 2, images, (height + 2) * width, GW), jnp.bfloat16),
            pltpu.VMEM((2, groups, 3 * GW, 3 * GW), jnp.float32),
            pltpu.VMEM((2, groups, taps_rows, GW), jnp.bfloat16),
            pltpu.VMEM((2, groups, taps_rows, GW), jnp.float32),
            pltpu.VMEM((max(shards - 1, 1), 2, groups, share, GW), jnp.bfloat16),
            dma((groups,)),
            dma((ticks - 1, groups, 2)),
            dma((1,)),
            dma((groups,)),
            pltpu.SemaphoreType.REGULAR,
            dma((max(shards - 1, 1), 2)),
            dma((max(shards - 1, 1), groups)),
        ],
        compiler_params=pltpu.CompilerParams(
            collective_id=0, has_side_effects=True, vmem_limit_bytes=56 * 1024 * 1024
        ),
    )(states, conv_kernels.reshape(2, 3, 3, GW, chans), feed)
    final, grads = pl.pallas_call(
        write_kernel,
        out_shape=(
            jax.ShapeDtypeStruct(final.shape, final.dtype),
            jax.ShapeDtypeStruct(grads.shape, grads.dtype),
        ),
        in_specs=[pl.BlockSpec(memory_space=pltpu.VMEM)] * 2,
        out_specs=[anywhere] * 2,
        scratch_shapes=[dma((2,))],
        compiler_params=pltpu.CompilerParams(vmem_limit_bytes=1024 * 1024),
    )(final, grads)
    return (
        final.reshape(section_states.shape),
        grads.reshape(1, 2, share, chans),
    )


def solution(mesh):
    return jax.shard_map(
        on_device,
        mesh=mesh,
        in_specs=(
            P("section", None, "dp", None, None, None),
            P("section", None, None, None),
            P(None, None, "dp", None, None, None),
        ),
        out_specs=(P("section", None, "dp", None, None, None), P("section", None, "dp", None)),
        check_vma=False,
    )
```

```python
import functools

import jax
import jax.numpy as jnp
from jax import lax
from jax.experimental import pallas as pl
from jax.experimental.pallas import tpu as pltpu
from jax.sharding import PartitionSpec as P

GW = 128
MESH = pl.DeviceIdType.MESH
PARTS = ((0, 1, 0), (3, 1, 0), (1, 2, 1))


def smooth_grad(value):
    sigma = jax.nn.sigmoid(value)
    return sigma * (1.0 + value * (1.0 - sigma))


def steps_in_order(groups, ticks):
    tuned = ((0, 0), (0, 1), (1, 0), (0, 2), (1, 1), (0, 3), (2, 0), (1, 2), (2, 1), (1, 3), (3, 0), (2, 2), (3, 1), (2, 3), (3, 2), (3, 3))
    if sorted(tuned) == [(group, tick) for group in range(groups) for tick in range(ticks)]:
        return tuned
    return [(group, tick) for tick in range(ticks) for group in range(groups)]


def fused_kernel(
    dims,
    states_ref,
    kernels_ref,
    feed_ref,
    final_ref,
    grads_ref,
    inbuf,
    outbuf,
    weights,
    flipped,
    padded,
    acc,
    gsend,
    gown,
    grecv,
    first_sem,
    in_sem,
    send_sem,
    weight_sem,
    turn_sem,
    gsend_sem,
    grecv_sem,
):
    ticks, groups, images, height, width, share, shards = dims
    cells = height * width
    order = steps_in_order(groups, ticks)
    rows = images * cells
    pad = (height + 2) * width
    me = lax.axis_index("section")
    count = lax.axis_size("section")
    mine = lax.axis_index("dp")
    is_top = me == count - 1
    lower = jnp.logical_and(me == 0, me < count - 1)
    upper = me == 1
    has_below = me > 0

    def lanes(group):
        start = group * GW
        return pl.ds(start if isinstance(group, int) else pl.multiple_of(start, GW), GW)

    def first_copy(group):
        return pltpu.make_async_copy(
            states_ref.at[:, :, lanes(group)], inbuf.at[0, group], first_sem.at[group]
        )

    def feed_copies(tick, group):
        for first, size, part in PARTS:
            yield pltpu.make_async_copy(
                feed_ref.at[tick - 1, pl.ds(first, size), :, lanes(group)],
                inbuf.at[tick, group, pl.ds(first, size)],
                in_sem.at[tick - 1, group, part],
            )

    def weight_copy(group, branch, column):
        row, place = ((0, 0), (0, 1), (3, 1))[column]
        return pltpu.make_async_copy(
            kernels_ref.at[branch, :, column, :, lanes(group)],
            weights.at[branch, group, pl.ds(row, 3), :, pl.ds(place * GW, GW)],
            weight_sem.at[group],
        )

    def weights_arrived(group):
        whole = kernels_ref.at[:, :, :, :, lanes(group)]
        pltpu.make_async_copy(whole, whole, weight_sem.at[group]).wait()

    def below_copy(tick, group, first, size, part):
        return pltpu.make_async_remote_copy(
            src_ref=outbuf.at[tick, group, pl.ds(first, size)],
            dst_ref=inbuf.at[tick + 1, group, pl.ds(first, size)],
            send_sem=send_sem.at[0],
            recv_sem=in_sem.at[tick, group, part],
            device_id={"section": me - 1},
            device_id_type=MESH,
        )

    def arrived(tick, group, part):
        pair = inbuf.at[tick, group, pl.ds(1, 2)]
        pltpu.make_async_copy(pair, pair, in_sem.at[tick - 1, group, part]).wait()

    def share_copy(group, branch, offset):
        partner = lax.rem(mine + offset, shards)
        return pltpu.make_async_remote_copy(
            src_ref=gsend.at[branch, group, pl.ds(pl.multiple_of(partner * share, 16), share)],
            dst_ref=grecv.at[offset - 1, branch, group],
            send_sem=gsend_sem.at[offset - 1, branch],
            recv_sem=grecv_sem.at[offset - 1, group],
            device_id={"dp": partner},
            device_id_type=MESH,
        )

    barrier = pltpu.get_barrier_semaphore()

    @pl.when(has_below)
    def _():
        pl.semaphore_signal(barrier, inc=1, device_id={"section": me - 1}, device_id_type=MESH)

    @pl.when(jnp.logical_not(is_top))
    def _():
        pl.semaphore_signal(barrier, inc=1, device_id={"section": me + 1}, device_id_type=MESH)

    for offset in range(1, shards):
        pl.semaphore_signal(
            barrier,
            inc=1,
            device_id={"dp": lax.rem(mine + offset, shards)},
            device_id_type=MESH,
        )

    for group in range(groups):
        first_copy(group).start()
        for branch in (1, 0):
            for column in range(3):
                weight_copy(group, branch, column).start()

    @pl.when(is_top)
    def _():
        @pl.loop(1, ticks)
        def _(tick):
            for group in range(groups):
                for copy in feed_copies(tick, group):
                    copy.start()

    edge = jnp.zeros((4, 2, images, width, GW), jnp.bfloat16)
    padded[:, :, :, 0:width, :] = edge
    padded[:, :, :, pad - width : pad, :] = edge
    blank = jnp.zeros((3, GW, GW), jnp.bfloat16)

    greeted = jnp.where(has_below, 1, 0) + jnp.where(is_top, 0, 1) + (shards - 1)
    column = lax.rem(lax.broadcasted_iota(jnp.int32, (rows, GW), 0), width)
    at_left = column == 0
    at_right = column == width - 1
    chunk = GW if rows % GW == 0 and GW % width == 0 else rows
    lane_column = lax.rem(lax.broadcasted_iota(jnp.int32, (GW, chunk), 1), width)
    lane_left = lane_column == 0
    lane_right = lane_column == width - 1

    def put(slot, field):
        wide = field.astype(jnp.float32)
        ahead = jnp.where(at_right, 0.0, pltpu.roll(wide, rows - 1, 0)).astype(jnp.bfloat16)
        for place, piece in enumerate((field, ahead)):
            padded[slot, place, :, width : width + cells, :] = piece.reshape(images, cells, GW)

    def slab(slot, places, order):
        return jnp.concatenate(
            [
                padded[slot, place, :, row * width : row * width + cells, :].reshape(rows, GW)
                for place in places
                for row in order
            ],
            axis=1,
        )

    def mix(slot, kernel):
        wide = lax.dot_general(
            slab(slot, (0, 1), (0, 1, 2)),
            kernel.reshape(6 * GW, 2 * GW),
            (((1,), (0,)), ((), ())),
            preferred_element_type=jnp.float32,
        )
        return wide[:, GW:] + jnp.where(at_left, 0.0, pltpu.roll(wide[:, :GW], 1, 0))

    def turned(field):
        flat = field.T
        parts = ([], [], [])
        for start in range(0, rows, chunk):
            piece = flat[:, start : start + chunk].astype(jnp.float32)
            left = jnp.where(lane_left, 0.0, pltpu.roll(piece, 1, 1))
            right = jnp.where(lane_right, 0.0, pltpu.roll(piece, chunk - 1, 1))
            parts[0].append(left.astype(jnp.bfloat16))
            parts[1].append(flat[:, start : start + chunk])
            parts[2].append(right.astype(jnp.bfloat16))
        return jnp.concatenate([jnp.concatenate(part, axis=1) for part in parts], axis=0)

    def term_of(field, slot):
        return lax.dot_general(
            turned(field),
            slab(slot, (0,), (2, 1, 0)),
            (((1,), (0,)), ((), ())),
            preferred_element_type=jnp.float32,
        )

    def hand_on(branch, group, field, slot):
        term = term_of(field, slot)
        for k in range(9):
            down, side = divmod(k, 3)
            here = (
                slice(side * GW, (side + 1) * GW),
                slice(down * GW, (down + 1) * GW),
            )
            block = (acc[(branch, group, *here)] + term[here]) * (1.0 / cells)
            gown[branch, group, k * GW : (k + 1) * GW, :] = block
            gsend[branch, group, k * GW : (k + 1) * GW, :] = block.astype(jnp.bfloat16)
        waiting = branch == 0 and shards > 1

        @pl.when(jnp.logical_or(not waiting, jnp.logical_or(me != 1, group < groups - 1)))
        def _():
            for offset in range(1, shards):
                share_copy(group, branch, offset).start()

    def prepare(branch, group):
        weights[branch, group, 3:6, :, 0:GW] = blank
        flipped[branch, group, 3:6, :, 0:GW] = blank
        for down in range(3):
            for side, (row, place) in enumerate(((0, 0), (0, 1), (3, 1))):
                from_row, from_place = ((0, 0), (0, 1), (3, 1))[2 - side]
                flipped[branch, group, row + down, :, place * GW : (place + 1) * GW] = weights[
                    branch, group, from_row + 2 - down, :, from_place * GW : (from_place + 1) * GW
                ].T

    def section(step, tick, group, first, last):
        def give(*copies):
            @pl.when(has_below)
            def _():
                for copy in copies:
                    below_copy(tick, group, *copy).start()

        def keep(stream, value):
            if last:
                final_ref[stream, :, lanes(group)] = value
            else:
                outbuf[tick, group, stream] = value

        def stream(at):
            return inbuf[tick, group, at].astype(jnp.float32)

        if first:
            first_copy(group).wait()
            weights_arrived(group)
        else:
            arrived(tick, group, 0)
        one = stream(0)
        act_one = jax.nn.silu(one).astype(jnp.bfloat16)
        put(0, act_one)
        put(1, inbuf[tick, group, 3])
        if last:
            hand_on(1, group, act_one, 1)
        mixed_one = mix(0, weights[1, group])
        if first:
            input_two = (stream(1) - mixed_one).astype(jnp.bfloat16)
            keep(1, input_two)

            @pl.when(step == 0)
            def _():
                pl.semaphore_wait(barrier, greeted)

            give((1, 1, 1))
            prepare(1, group)
        mixed_two = mix(1, flipped[1, group]) * smooth_grad(one)
        if not first:
            arrived(tick, group, 1)
            input_two = (stream(1) - mixed_one).astype(jnp.bfloat16)
            keep(1, input_two)
        total_one = (stream(2) + mixed_two).astype(jnp.bfloat16)
        keep(2, total_one)
        if first:
            give((2, 1, 1))
            prepare(0, group)
        wide_two = input_two.astype(jnp.float32)
        act_two = jax.nn.silu(wide_two).astype(jnp.bfloat16)
        put(2, act_two)
        put(3, total_one)
        if last:
            hand_on(0, group, act_two, 3)
        keep(0, (stream(0) - mix(2, weights[0, group])).astype(jnp.bfloat16))
        keep(
            3,
            (stream(3) + mix(3, flipped[0, group]) * smooth_grad(wide_two)).astype(jnp.bfloat16),
        )
        if first:
            give((0, 1, 0), (3, 1, 0))
            acc[1, group] = term_of(act_one, 1)
            acc[0, group] = term_of(act_two, 3)
        elif not last:
            give((0, 1, 0), (3, 1, 0), (1, 2, 1))
            acc[1, group] += term_of(act_one, 1)
            acc[0, group] += term_of(act_two, 3)

    @pl.loop(0, ticks * groups)
    def _(step):
        word = jnp.int32(0)
        for place in range(0, len(order), 3):
            packed = 0
            for at, (at_group, at_tick) in enumerate(order[place : place + 3]):
                packed |= (at_group * 32 + at_tick) << (10 * at)
            word = jnp.where(step >= place, packed, word)
        entry = lax.shift_right_logical(word, 10 * lax.rem(step, 3))
        tick = entry & 31
        group = lax.shift_right_logical(entry, 5) & 31

        @pl.when(tick == 0)
        def _():
            section(step, 0, group, True, False)

        @pl.when(jnp.logical_and(tick > 0, tick < ticks - 1))
        def _():
            section(step, tick, group, False, False)

        @pl.when(tick == ticks - 1)
        def _():
            section(step, ticks - 1, group, False, True)

    def shared(branch):
        for offset in range(1, shards):
            every = gsend.at[branch, :, pl.ds(0, share)]
            pltpu.make_async_copy(every, every, gsend_sem.at[offset - 1, branch]).wait()

    if shards > 1:

        @pl.when(upper)
        def _():
            pl.semaphore_wait(turn_sem, 1)
            for offset in range(1, shards):
                share_copy(groups - 1, 0, offset).start()

        shared(1)

        @pl.when(lower)
        def _():
            pl.semaphore_signal(turn_sem, inc=1, device_id={"section": me + 1}, device_id_type=MESH)

    @pl.loop(0, groups)
    def _(group):
        for offset in range(1, shards):
            both = grecv.at[offset - 1, :, group]
            pltpu.make_async_copy(both, both, grecv_sem.at[offset - 1, group]).wait()
        for branch in (1, 0):
            total = gown[branch, group, pl.ds(pl.multiple_of(mine * share, 16), share), :]
            for offset in range(1, shards):
                total = total + grecv[offset - 1, branch, group].astype(jnp.float32)
            grads_ref[branch, :, lanes(group)] = total

    shared(0)

    @pl.when(has_below)
    def _():
        every = outbuf.at[pl.ds(0, ticks - 1)]
        pltpu.make_async_copy(every, every, send_sem.at[0]).wait()


def write_kernel(final_ref, grads_ref, final_out, grads_out, sems):
    copies = [
        pltpu.make_async_copy(grads_ref, grads_out, sems.at[0]),
        pltpu.make_async_copy(final_ref, final_out, sems.at[1]),
    ]
    for copy in copies:
        copy.start()
    for copy in copies:
        copy.wait()


def on_device(section_states, conv_kernels, top_feed):
    _, _, images, height, width, chans = section_states.shape
    ticks = top_feed.shape[0] + 1
    groups = chans // GW
    shards = lax.axis_size("dp")
    taps_rows = conv_kernels.shape[2]
    share = taps_rows // shards
    rows = images * height * width
    states = section_states.reshape(4, rows, chans)
    feed = top_feed.reshape(ticks - 1, 4, rows, chans)
    dims = (ticks, groups, images, height, width, share, shards)
    anywhere = pl.BlockSpec(memory_space=pltpu.HBM)
    dma = pltpu.SemaphoreType.DMA
    final, grads = pl.pallas_call(
        functools.partial(fused_kernel, dims),
        out_shape=(
            pltpu.VMEM((4, rows, chans), jnp.bfloat16),
            pltpu.VMEM((2, share, chans), jnp.float32),
        ),
        in_specs=[anywhere] * 3,
        out_specs=[pl.BlockSpec(memory_space=pltpu.VMEM)] * 2,
        scratch_shapes=[
            pltpu.VMEM((ticks, groups, 4, rows, GW), jnp.bfloat16),
            pltpu.VMEM((ticks, groups, 4, rows, GW), jnp.bfloat16),
            pltpu.VMEM((2, groups, 6, GW, 2 * GW), jnp.bfloat16),
            pltpu.VMEM((2, groups, 6, GW, 2 * GW), jnp.bfloat16),
            pltpu.VMEM((4, 2, images, (height + 2) * width, GW), jnp.bfloat16),
            pltpu.VMEM((2, groups, 3 * GW, 3 * GW), jnp.float32),
            pltpu.VMEM((2, groups, taps_rows, GW), jnp.bfloat16),
            pltpu.VMEM((2, groups, taps_rows, GW), jnp.float32),
            pltpu.VMEM((max(shards - 1, 1), 2, groups, share, GW), jnp.bfloat16),
            dma((groups,)),
            dma((ticks - 1, groups, 2)),
            dma((1,)),
            dma((groups,)),
            pltpu.SemaphoreType.REGULAR,
            dma((max(shards - 1, 1), 2)),
            dma((max(shards - 1, 1), groups)),
        ],
        compiler_params=pltpu.CompilerParams(
            collective_id=0, has_side_effects=True, vmem_limit_bytes=56 * 1024 * 1024
        ),
    )(states, conv_kernels.reshape(2, 3, 3, GW, chans), feed)
    final, grads = pl.pallas_call(
        write_kernel,
        out_shape=(
            jax.ShapeDtypeStruct(final.shape, final.dtype),
            jax.ShapeDtypeStruct(grads.shape, grads.dtype),
        ),
        in_specs=[pl.BlockSpec(memory_space=pltpu.VMEM)] * 2,
        out_specs=[anywhere] * 2,
        scratch_shapes=[dma((2,))],
        compiler_params=pltpu.CompilerParams(vmem_limit_bytes=1024 * 1024),
    )(final, grads)
    return (
        final.reshape(section_states.shape),
        grads.reshape(1, 2, share, chans),
    )


def solution(mesh):
    return jax.shard_map(
        on_device,
        mesh=mesh,
        in_specs=(
            P("section", None, "dp", None, None, None),
            P("section", None, None, None),
            P(None, None, "dp", None, None, None),
        ),
        out_specs=(P("section", None, "dp", None, None, None), P("section", None, "dp", None)),
        check_vma=False,
    )
```

```python
import functools

import jax
import jax.numpy as jnp
from jax import lax
from jax.experimental import pallas as pl
from jax.experimental.pallas import tpu as pltpu
from jax.sharding import PartitionSpec as P

GW = 128
MESH = pl.DeviceIdType.MESH
PARTS = ((0, 1, 0), (3, 1, 0), (1, 2, 1))


def smooth_grad(value):
    sigma = jax.nn.sigmoid(value)
    return sigma * (1.0 + value * (1.0 - sigma))


def steps_in_order(groups, ticks):
    tuned = ((0, 0), (0, 1), (1, 0), (0, 2), (1, 1), (2, 0), (0, 3), (1, 2), (2, 1), (1, 3), (3, 0), (2, 2), (3, 1), (2, 3), (3, 2), (3, 3))
    if sorted(tuned) == [(group, tick) for group in range(groups) for tick in range(ticks)]:
        return tuned
    return [(group, tick) for tick in range(ticks) for group in range(groups)]


def fused_kernel(
    dims,
    states_ref,
    kernels_ref,
    feed_ref,
    final_ref,
    grads_ref,
    inbuf,
    outbuf,
    weights,
    flipped,
    padded,
    acc,
    gsend,
    gown,
    grecv,
    first_sem,
    in_sem,
    send_sem,
    weight_sem,
    turn_sem,
    gsend_sem,
    grecv_sem,
):
    ticks, groups, images, height, width, share, shards = dims
    cells = height * width
    order = steps_in_order(groups, ticks)
    rows = images * cells
    pad = (height + 2) * width
    me = lax.axis_index("section")
    count = lax.axis_size("section")
    mine = lax.axis_index("dp")
    is_top = me == count - 1
    lower = jnp.logical_and(lax.rem(me, 2) == 0, me < count - 1)
    upper = lax.rem(me, 2) == 1
    has_below = me > 0

    def lanes(group):
        start = group * GW
        return pl.ds(start if isinstance(group, int) else pl.multiple_of(start, GW), GW)

    def first_copy(group):
        return pltpu.make_async_copy(
            states_ref.at[:, :, lanes(group)], inbuf.at[0, group], first_sem.at[group]
        )

    def feed_copies(tick, group):
        for first, size, part in PARTS:
            yield pltpu.make_async_copy(
                feed_ref.at[tick - 1, pl.ds(first, size), :, lanes(group)],
                inbuf.at[tick, group, pl.ds(first, size)],
                in_sem.at[tick - 1, group, part],
            )

    def weight_copy(group, branch, column):
        row, place = ((0, 0), (0, 1), (3, 1))[column]
        return pltpu.make_async_copy(
            kernels_ref.at[branch, :, column, :, lanes(group)],
            weights.at[branch, group, pl.ds(row, 3), :, pl.ds(place * GW, GW)],
            weight_sem.at[group],
        )

    def weights_arrived(group):
        whole = kernels_ref.at[:, :, :, :, lanes(group)]
        pltpu.make_async_copy(whole, whole, weight_sem.at[group]).wait()

    def below_copy(tick, group, first, size, part):
        return pltpu.make_async_remote_copy(
            src_ref=outbuf.at[tick, group, pl.ds(first, size)],
            dst_ref=inbuf.at[tick + 1, group, pl.ds(first, size)],
            send_sem=send_sem.at[0],
            recv_sem=in_sem.at[tick, group, part],
            device_id={"section": me - 1},
            device_id_type=MESH,
        )

    def arrived(tick, group, part):
        pair = inbuf.at[tick, group, pl.ds(1, 2)]
        pltpu.make_async_copy(pair, pair, in_sem.at[tick - 1, group, part]).wait()

    def share_copy(group, branch, offset):
        partner = lax.rem(mine + offset, shards)
        return pltpu.make_async_remote_copy(
            src_ref=gsend.at[branch, group, pl.ds(pl.multiple_of(partner * share, 16), share)],
            dst_ref=grecv.at[offset - 1, branch, group],
            send_sem=gsend_sem.at[offset - 1, branch],
            recv_sem=grecv_sem.at[offset - 1, group],
            device_id={"dp": partner},
            device_id_type=MESH,
        )

    barrier = pltpu.get_barrier_semaphore()

    @pl.when(has_below)
    def _():
        pl.semaphore_signal(barrier, inc=1, device_id={"section": me - 1}, device_id_type=MESH)

    @pl.when(jnp.logical_not(is_top))
    def _():
        pl.semaphore_signal(barrier, inc=1, device_id={"section": me + 1}, device_id_type=MESH)

    for offset in range(1, shards):
        pl.semaphore_signal(
            barrier,
            inc=1,
            device_id={"dp": lax.rem(mine + offset, shards)},
            device_id_type=MESH,
        )

    for group in range(groups):
        first_copy(group).start()
        for branch in (1, 0):
            for column in range(3):
                weight_copy(group, branch, column).start()

    @pl.when(is_top)
    def _():
        @pl.loop(1, ticks)
        def _(tick):
            for group in range(groups):
                for copy in feed_copies(tick, group):
                    copy.start()

    edge = jnp.zeros((4, 2, images, width, GW), jnp.bfloat16)
    padded[:, :, :, 0:width, :] = edge
    padded[:, :, :, pad - width : pad, :] = edge
    blank = jnp.zeros((3, GW, GW), jnp.bfloat16)

    greeted = jnp.where(has_below, 1, 0) + jnp.where(is_top, 0, 1) + (shards - 1)
    column = lax.rem(lax.broadcasted_iota(jnp.int32, (rows, GW), 0), width)
    at_left = column == 0
    at_right = column == width - 1
    chunk = GW if rows % GW == 0 and GW % width == 0 else rows
    lane_column = lax.rem(lax.broadcasted_iota(jnp.int32, (GW, chunk), 1), width)
    lane_left = lane_column == 0
    lane_right = lane_column == width - 1

    def put(slot, field):
        wide = field.astype(jnp.float32)
        ahead = jnp.where(at_right, 0.0, pltpu.roll(wide, rows - 1, 0)).astype(jnp.bfloat16)
        for place, piece in enumerate((field, ahead)):
            padded[slot, place, :, width : width + cells, :] = piece.reshape(images, cells, GW)

    def slab(slot, places, order):
        return jnp.concatenate(
            [
                padded[slot, place, :, row * width : row * width + cells, :].reshape(rows, GW)
                for place in places
                for row in order
            ],
            axis=1,
        )

    def mix(slot, kernel):
        wide = lax.dot_general(
            slab(slot, (0, 1), (0, 1, 2)),
            kernel.reshape(6 * GW, 2 * GW),
            (((1,), (0,)), ((), ())),
            preferred_element_type=jnp.float32,
        )
        return wide[:, GW:] + jnp.where(at_left, 0.0, pltpu.roll(wide[:, :GW], 1, 0))

    def turned(field):
        flat = field.T
        parts = ([], [], [])
        for start in range(0, rows, chunk):
            piece = flat[:, start : start + chunk].astype(jnp.float32)
            left = jnp.where(lane_left, 0.0, pltpu.roll(piece, 1, 1))
            right = jnp.where(lane_right, 0.0, pltpu.roll(piece, chunk - 1, 1))
            parts[0].append(left.astype(jnp.bfloat16))
            parts[1].append(flat[:, start : start + chunk])
            parts[2].append(right.astype(jnp.bfloat16))
        return jnp.concatenate([jnp.concatenate(part, axis=1) for part in parts], axis=0)

    def term_of(field, slot):
        return lax.dot_general(
            turned(field),
            slab(slot, (0,), (2, 1, 0)),
            (((1,), (0,)), ((), ())),
            preferred_element_type=jnp.float32,
        )

    def hand_on(branch, group, field, slot):
        term = term_of(field, slot)
        for k in range(9):
            down, side = divmod(k, 3)
            here = (
                slice(side * GW, (side + 1) * GW),
                slice(down * GW, (down + 1) * GW),
            )
            block = (acc[(branch, group, *here)] + term[here]) * (1.0 / cells)
            gown[branch, group, k * GW : (k + 1) * GW, :] = block
            gsend[branch, group, k * GW : (k + 1) * GW, :] = block.astype(jnp.bfloat16)
        waiting = branch == 0 and shards > 1

        @pl.when(jnp.logical_or(not waiting, jnp.logical_or(lax.rem(me, 2) == 0, group < groups - 1)))
        def _():
            for offset in range(1, shards):
                share_copy(group, branch, offset).start()

    def prepare(branch, group):
        weights[branch, group, 3:6, :, 0:GW] = blank
        flipped[branch, group, 3:6, :, 0:GW] = blank
        for down in range(3):
            for side, (row, place) in enumerate(((0, 0), (0, 1), (3, 1))):
                from_row, from_place = ((0, 0), (0, 1), (3, 1))[2 - side]
                flipped[branch, group, row + down, :, place * GW : (place + 1) * GW] = weights[
                    branch, group, from_row + 2 - down, :, from_place * GW : (from_place + 1) * GW
                ].T

    def section(step, tick, group, first, last):
        def give(*copies):
            @pl.when(has_below)
            def _():
                for copy in copies:
                    below_copy(tick, group, *copy).start()

        def keep(stream, value):
            if last:
                final_ref[stream, :, lanes(group)] = value
            else:
                outbuf[tick, group, stream] = value

        def stream(at):
            return inbuf[tick, group, at].astype(jnp.float32)

        if first:
            first_copy(group).wait()
            weights_arrived(group)
        else:
            arrived(tick, group, 0)
        one = stream(0)
        act_one = jax.nn.silu(one).astype(jnp.bfloat16)
        put(0, act_one)
        put(1, inbuf[tick, group, 3])
        if last:
            hand_on(1, group, act_one, 1)
        mixed_one = mix(0, weights[1, group])
        if first:
            input_two = (stream(1) - mixed_one).astype(jnp.bfloat16)
            keep(1, input_two)

            @pl.when(step == 0)
            def _():
                pl.semaphore_wait(barrier, greeted)

            give((1, 1, 1))
            prepare(1, group)
        mixed_two = mix(1, flipped[1, group]) * smooth_grad(one)
        if not first:
            arrived(tick, group, 1)
            input_two = (stream(1) - mixed_one).astype(jnp.bfloat16)
            keep(1, input_two)
        total_one = (stream(2) + mixed_two).astype(jnp.bfloat16)
        keep(2, total_one)
        if first:
            give((2, 1, 1))
            prepare(0, group)
        wide_two = input_two.astype(jnp.float32)
        act_two = jax.nn.silu(wide_two).astype(jnp.bfloat16)
        put(2, act_two)
        put(3, total_one)
        if last:
            hand_on(0, group, act_two, 3)
        keep(0, (stream(0) - mix(2, weights[0, group])).astype(jnp.bfloat16))
        keep(
            3,
            (stream(3) + mix(3, flipped[0, group]) * smooth_grad(wide_two)).astype(jnp.bfloat16),
        )
        if first:
            give((0, 1, 0), (3, 1, 0))
            acc[1, group] = term_of(act_one, 1)
            acc[0, group] = term_of(act_two, 3)
        elif not last:
            give((0, 1, 0), (3, 1, 0), (1, 2, 1))
            acc[1, group] += term_of(act_one, 1)
            acc[0, group] += term_of(act_two, 3)

    @pl.loop(0, ticks * groups)
    def _(step):
        word = jnp.int32(0)
        for place in range(0, len(order), 3):
            packed = 0
            for at, (at_group, at_tick) in enumerate(order[place : place + 3]):
                packed |= (at_group * 32 + at_tick) << (10 * at)
            word = jnp.where(step >= place, packed, word)
        entry = lax.shift_right_logical(word, 10 * lax.rem(step, 3))
        tick = entry & 31
        group = lax.shift_right_logical(entry, 5) & 31

        @pl.when(tick == 0)
        def _():
            section(step, 0, group, True, False)

        @pl.when(jnp.logical_and(tick > 0, tick < ticks - 1))
        def _():
            section(step, tick, group, False, False)

        @pl.when(tick == ticks - 1)
        def _():
            section(step, ticks - 1, group, False, True)

    def shared(branch):
        for offset in range(1, shards):
            every = gsend.at[branch, :, pl.ds(0, share)]
            pltpu.make_async_copy(every, every, gsend_sem.at[offset - 1, branch]).wait()

    if shards > 1:

        @pl.when(upper)
        def _():
            pl.semaphore_wait(turn_sem, 1)
            for offset in range(1, shards):
                share_copy(groups - 1, 0, offset).start()

        shared(1)

        @pl.when(lower)
        def _():
            pl.semaphore_signal(turn_sem, inc=1, device_id={"section": me + 1}, device_id_type=MESH)

    @pl.loop(0, groups)
    def _(group):
        for offset in range(1, shards):
            both = grecv.at[offset - 1, :, group]
            pltpu.make_async_copy(both, both, grecv_sem.at[offset - 1, group]).wait()
        for branch in (1, 0):
            total = gown[branch, group, pl.ds(pl.multiple_of(mine * share, 16), share), :]
            for offset in range(1, shards):
                total = total + grecv[offset - 1, branch, group].astype(jnp.float32)
            grads_ref[branch, :, lanes(group)] = total

    shared(0)

    @pl.when(has_below)
    def _():
        every = outbuf.at[pl.ds(0, ticks - 1)]
        pltpu.make_async_copy(every, every, send_sem.at[0]).wait()


def write_kernel(final_ref, grads_ref, final_out, grads_out, sems):
    copies = [
        pltpu.make_async_copy(grads_ref, grads_out, sems.at[0]),
        pltpu.make_async_copy(final_ref, final_out, sems.at[1]),
    ]
    for copy in copies:
        copy.start()
    for copy in copies:
        copy.wait()


def on_device(section_states, conv_kernels, top_feed):
    _, _, images, height, width, chans = section_states.shape
    ticks = top_feed.shape[0] + 1
    groups = chans // GW
    shards = lax.axis_size("dp")
    taps_rows = conv_kernels.shape[2]
    share = taps_rows // shards
    rows = images * height * width
    states = section_states.reshape(4, rows, chans)
    feed = top_feed.reshape(ticks - 1, 4, rows, chans)
    dims = (ticks, groups, images, height, width, share, shards)
    anywhere = pl.BlockSpec(memory_space=pltpu.HBM)
    dma = pltpu.SemaphoreType.DMA
    final, grads = pl.pallas_call(
        functools.partial(fused_kernel, dims),
        out_shape=(
            pltpu.VMEM((4, rows, chans), jnp.bfloat16),
            pltpu.VMEM((2, share, chans), jnp.float32),
        ),
        in_specs=[anywhere] * 3,
        out_specs=[pl.BlockSpec(memory_space=pltpu.VMEM)] * 2,
        scratch_shapes=[
            pltpu.VMEM((ticks, groups, 4, rows, GW), jnp.bfloat16),
            pltpu.VMEM((ticks, groups, 4, rows, GW), jnp.bfloat16),
            pltpu.VMEM((2, groups, 6, GW, 2 * GW), jnp.bfloat16),
            pltpu.VMEM((2, groups, 6, GW, 2 * GW), jnp.bfloat16),
            pltpu.VMEM((4, 2, images, (height + 2) * width, GW), jnp.bfloat16),
            pltpu.VMEM((2, groups, 3 * GW, 3 * GW), jnp.float32),
            pltpu.VMEM((2, groups, taps_rows, GW), jnp.bfloat16),
            pltpu.VMEM((2, groups, taps_rows, GW), jnp.float32),
            pltpu.VMEM((max(shards - 1, 1), 2, groups, share, GW), jnp.bfloat16),
            dma((groups,)),
            dma((ticks - 1, groups, 2)),
            dma((1,)),
            dma((groups,)),
            pltpu.SemaphoreType.REGULAR,
            dma((max(shards - 1, 1), 2)),
            dma((max(shards - 1, 1), groups)),
        ],
        compiler_params=pltpu.CompilerParams(
            collective_id=0, has_side_effects=True, vmem_limit_bytes=56 * 1024 * 1024
        ),
    )(states, conv_kernels.reshape(2, 3, 3, GW, chans), feed)
    final, grads = pl.pallas_call(
        write_kernel,
        out_shape=(
            jax.ShapeDtypeStruct(final.shape, final.dtype),
            jax.ShapeDtypeStruct(grads.shape, grads.dtype),
        ),
        in_specs=[pl.BlockSpec(memory_space=pltpu.VMEM)] * 2,
        out_specs=[anywhere] * 2,
        scratch_shapes=[dma((2,))],
        compiler_params=pltpu.CompilerParams(vmem_limit_bytes=1024 * 1024),
    )(final, grads)
    return (
        final.reshape(section_states.shape),
        grads.reshape(1, 2, share, chans),
    )


def solution(mesh):
    return jax.shard_map(
        on_device,
        mesh=mesh,
        in_specs=(
            P("section", None, "dp", None, None, None),
            P("section", None, None, None),
            P(None, None, "dp", None, None, None),
        ),
        out_specs=(P("section", None, "dp", None, None, None), P("section", None, "dp", None)),
        check_vma=False,
    )
```
